256 devices in a mesh: row: 32 (over z, x_lo, core), col: 8 (over y, x_hi).
Axes of the slice: x: 4 (x_hi: 2, x_lo: 2; x = x_hi * 2 + x_lo), y: 4, z: 8, core: 2. Of those that a mesh axis runs over, the one named last changes fastest.
Arguments:
- vectors: bfloat16 [8, 262144], P(None, ('row', 'col')), may hold values from -6 to 6
- energies: float32 [262144], P(('row', 'col')), may hold values from 0.5 to 6
- tiles: bfloat16 [262144, 4096], P(('row', 'col')), may hold values from -0.25 to 0.25
- tile_rows: int32 [262144], P(('row', 'col')), may hold values from 0 to 127, as said below
- tile_cols: int32 [262144], P(('row', 'col')), may hold values from 0 to 511
- tile_count: int32 [256], P(('row', 'col')), may hold values from 128 to 1024, as said below
Outputs:
- product: bfloat16 [8, 262144], P(None, ('row', 'col'))
- residual: float32 [8, 262144], P(None, ('row', 'col'))
The draws below stay inside these ranges and needn't reach their ends.
Inputs may be any that keep to these rules, and one draw needn't show every extreme that they name: `tile_count`: every count is at least 128, and some device uses all 1024 slots in every draw; a few devices are full while most use far fewer. `tile_rows`: slots may name the same row and column block more than once; such tiles add.
All inputs are finite; a program needn't handle non-finite values.
Results may differ from the reference program's by a relative error of at most 0.008.
Values may be sent and summed in bfloat16 or wider, within the bound.
A program may use at most 64 MiB of HBM per device.

```python
import jax
import jax.numpy as jnp
from jax import lax

K = 8
BLK_DEV = 16
TILE_DEV = 1024
NBLK = 4096
NBASIS = 262144
SLOTS = 262144
N_ROW = 32
N_COL = 8


def draw_energies(key, part):
    base = 1.0 + 2.0 * jnp.arange(NBASIS, dtype=jnp.float32) / NBASIS
    factor = jnp.exp(jax.random.uniform(key, (NBASIS,), jnp.float32, -0.6, 0.6))
    return jnp.clip(base * factor, 0.5, 6.0)


def draw_tile_count(key, part):
    first = jax.random.fold_in(key, 11)
    second = jax.random.fold_in(key, 23)
    counts = jax.random.randint(first, (N_ROW * N_COL,), TILE_DEV // 8, TILE_DEV // 2 + 1)
    heavy = jax.random.randint(second, (4,), 0, N_ROW * N_COL)
    return counts.at[heavy].set(TILE_DEV).astype(jnp.int32)


def tile_layout(key):
    devices = N_ROW * N_COL
    key_rows = jax.random.fold_in(key, 41)
    key_cols = jax.random.fold_in(key, 43)
    key_own = jax.random.fold_in(key, 47)
    key_pick = jax.random.fold_in(key, 53)
    rows = jax.random.randint(key_rows, (devices, TILE_DEV), 0, N_COL * BLK_DEV)
    cols = jax.random.randint(key_cols, (devices, TILE_DEV), 0, N_ROW * BLK_DEV)
    own_block = jax.random.randint(key_own, (devices, TILE_DEV), 0, BLK_DEV)
    picked = jax.random.randint(key_pick, (devices, TILE_DEV), 0, 4) == 0
    device = jnp.arange(devices, dtype=jnp.int32)[:, None]
    row_index = device // N_COL
    col_index = device % N_COL
    rows = jnp.where(picked, col_index * BLK_DEV + own_block, rows)
    cols = jnp.where(picked, row_index * BLK_DEV + own_block, cols)
    return (rows.reshape(-1).astype(jnp.int32), cols.reshape(-1).astype(jnp.int32))


def draw_tile_rows(key, part):
    rows, cols = tile_layout(key)
    return rows


def draw_tile_cols(key, part):
    rows, cols = tile_layout(key)
    return cols


def draw_tiles(key, part):
    scale = (64.0 * TILE_DEV / BLK_DEV) ** (-0.5)
    key_base = jax.random.fold_in(key, 61)
    key_bias = jax.random.fold_in(key, 67)
    base = jnp.clip(jax.random.normal(key_base, (SLOTS, 64, 64), jnp.float32), -6.0, 6.0)
    bias = jax.random.uniform(key_bias, (SLOTS, 1, 1), jnp.float32, 0.03, 0.08)
    diagonal_mask = (jnp.arange(64)[:, None] == jnp.arange(64)[None, :]).astype(jnp.float32)
    return jnp.clip(scale * base + bias * diagonal_mask[None, :, :], -0.25, 0.25).reshape(SLOTS, 4096).astype(jnp.bfloat16)


def block_scale(stream_key, extent, cuts, least, largest):
    factor_of, own = 1.0, jax.random.fold_in(stream_key, 6)
    for axis_at, parts in cuts:
        draws = jnp.exp(jax.random.uniform(jax.random.fold_in(own, axis_at), (parts,), jnp.float32, least / len(cuts), largest / len(cuts)))
        factor_of = factor_of * jnp.repeat(draws, extent[axis_at] // parts).reshape([-1 if axis == axis_at else 1 for axis in range(len(extent))])
    return factor_of


def normal_values(rng, dims, scale, bound, cuts=(), kind=jnp.bfloat16):
    result = jax.random.normal(rng, dims, jnp.float32) * scale
    if len(cuts) > 0:
        result = block_scale(rng, dims, cuts, -0.22, 0.18) * result
    return jnp.clip(result, min=-bound, max=bound).astype(kind)


def setup_inputs(seed: int = 0) -> dict:
    seeds = jax.random.split(jax.random.key(seed), 7)
    return {
        "vectors": normal_values(seeds[0], (K, NBASIS), 1.0, 6.0, ((1, 256),)),
        "energies": draw_energies(jax.random.fold_in(seeds[6], 71), 0),
        "tiles": draw_tiles(jax.random.fold_in(seeds[6], 71), 0),
        "tile_rows": draw_tile_rows(jax.random.fold_in(seeds[6], 71), 0),
        "tile_cols": draw_tile_cols(jax.random.fold_in(seeds[6], 71), 0),
        "tile_count": draw_tile_count(jax.random.fold_in(seeds[6], 71), 0),
    }


def reference(vectors, energies, tiles, tile_rows, tile_cols, tile_count):
    kvec = vectors.shape[0]
    blocks = vectors.reshape(kvec, NBLK, 64).astype(jnp.float32)
    tiles_dev = tiles.reshape(N_ROW * N_COL, TILE_DEV, 64, 64)
    rows_dev = tile_rows.reshape(N_ROW * N_COL, TILE_DEV)
    cols_dev = tile_cols.reshape(N_ROW * N_COL, TILE_DEV)
    device_ids = jnp.arange(N_ROW * N_COL, dtype=jnp.int32)
    slot_ids = jnp.arange(TILE_DEV, dtype=jnp.int32)

    def one_device(accum, item):
        tile, local_rows, local_cols, count, device = item
        row_index = device // N_COL
        col_index = device % N_COL
        grow = (row_index * N_COL * BLK_DEV + local_rows).astype(jnp.int32)
        gcol = (((local_cols // BLK_DEV) * N_COL + col_index) * BLK_DEV + local_cols % BLK_DEV).astype(jnp.int32)
        gathered = blocks[:, gcol, :]
        prod = jnp.einsum("tji,kti->ktj", tile.astype(jnp.float32), gathered, precision=lax.Precision.HIGHEST)
        live = (slot_ids < count).astype(jnp.float32)
        prod = prod * live[None, :, None]
        return accum.at[:, grow, :].add(prod), None

    start = jnp.zeros((kvec, NBLK, 64), jnp.float32)
    off, _ = lax.scan(one_device, start, (tiles_dev, rows_dev, cols_dev, tile_count, device_ids))
    vec32 = vectors.astype(jnp.float32)
    whole = energies[None, :] * vec32 + off.reshape(kvec, NBASIS)
    gram = jnp.einsum("an,bn->ab", vec32, whole, precision=lax.Precision.HIGHEST) / NBASIS
    residual = whole - jnp.einsum("ab,an->bn", gram, vec32, precision=lax.Precision.HIGHEST)
    return whole.astype(jnp.bfloat16), residual
```

```python
import jax
import jax.numpy as jnp
from jax import lax
from jax.experimental import pallas as pl
from jax.experimental.pallas import tpu as pltpu
from jax.sharding import PartitionSpec as P

F32, BF16 = jnp.float32, jnp.bfloat16
NEAR_LAST = (4, 3, 5, 2, 6, 1, 7)
NEAR_FIRST = (1, 7, 2, 6, 3, 5, 4)


def iota(shape, dim):
    return lax.broadcasted_iota(jnp.int32, shape, dim)


def low_half():
    return iota((1, 128), 1) < 64


def turn(value):
    return pltpu.roll(value, 64, 1)


def to_blocks(natural, out_ref):
    low = low_half()
    for t in range(8):
        part = natural[:, 128 * t : 128 * t + 128]
        turned = turn(part)
        for p in range(4):
            a, b = 2 * p, 2 * p + 1
            lanes = pl.ds(128 * p, 128)
            out_ref[pl.ds(2 * t, 1), lanes] = jnp.where(low, part[a : a + 1], turned[b : b + 1])
            out_ref[pl.ds(2 * t + 1, 1), lanes] = jnp.where(low, turned[a : a + 1], part[b : b + 1])


def from_blocks(value, p, out_ref):
    low = low_half()
    turned = turn(value)
    for t in range(8):
        a, b = 2 * t, 2 * t + 1
        lanes = pl.ds(128 * t, 128)
        out_ref[pl.ds(2 * p, 1), lanes] = jnp.where(low, value[a : a + 1], turned[b : b + 1])
        out_ref[pl.ds(2 * p + 1, 1), lanes] = jnp.where(low, turned[a : a + 1], value[b : b + 1])


def onehots(rows_ref, cols_ref, count_ref, rowhot, colhot, foldhot):
    count = count_ref[0]
    slot = iota((8, 128), 0) * 128 + iota((8, 128), 1)
    rows = jnp.where(slot < count, rows_ref[...], -1)
    cols = jnp.transpose(cols_ref[...].astype(F32))
    row_ids = iota((128, 128), 0)
    col_ids = iota((128, 512), 1).astype(F32)
    for t in range(8):
        hot = row_ids == rows[t : t + 1, :]
        rowhot[:, 128 * t : 128 * t + 128] = jnp.where(hot, 1.0, 0.0).astype(BF16)
        hot = cols[:, t : t + 1] == col_ids
        colhot[t] = jnp.where(hot, 1.0, 0.0).astype(BF16)
    lane = iota((256, 128), 1)
    spot = 2 * (iota((256, 128), 0) // 8)
    for jp in range(2):
        for kp in range(2):
            hot = lane == spot + (64 * kp + jp)
            foldhot[2 * jp + kp] = jnp.where(hot, 1.0, 0.0).astype(BF16)


def products(t, colhot, picked_from, tile_ref, y_ref):
    low = low_half()
    x = jnp.dot(colhot[t], picked_from, preferred_element_type=F32)
    parts = []
    for jp in range(2):
        keep = low if jp == 0 else jnp.logical_not(low)
        for k in range(8):
            value = x[:, 128 * (k // 2) : 128 * (k // 2) + 128]
            if k % 2 != jp:
                value = turn(value)
            parts.append(jnp.where(keep, value, 0.0))
    own = iota((8, 256), 1) % 8 == iota((8, 256), 0)
    outs = []
    for g in range(16):
        left = jnp.concatenate([part[8 * g : 8 * g + 8] for part in parts], axis=0).astype(BF16)
        right = tile_ref[t, pl.ds(256 * g, 256), :]
        outs.append(
            lax.dot_general(left, right, (((1,), (1,)), ((), ())), preferred_element_type=F32)
        )
        if g % 2 == 1:
            first = pl.multiple_of(128 * t + 8 * (g - 1), 16)
            for m in range(16):
                pair = [jnp.where(own, o[8 * m : 8 * m + 8], 0.0) for o in outs]
                y_ref[m, pl.ds(first, 16), :] = jnp.concatenate(pair, axis=0).astype(BF16)
            outs = []


def scattered(p, rowhot, y_ref, foldhot):
    hots = rowhot[...]
    total = jnp.zeros((128, 128), F32)
    for jp in range(2):
        for kp in range(2):
            acc = jnp.dot(hots, y_ref[8 * jp + 2 * p + kp], preferred_element_type=F32)
            upper = acc.astype(BF16)
            lower = (acc - upper.astype(F32)).astype(BF16)
            fold = foldhot[2 * jp + kp]
            total = total + jnp.dot(upper, fold, preferred_element_type=F32)
            total = total + jnp.dot(lower, fold, preferred_element_type=F32)
    return total


def kernel(
    n_states,
    vectors_ref,
    energies_ref,
    tiles_ref,
    rows_ref,
    cols_ref,
    count_ref,
    product_ref,
    residual_ref,
    tile_vm,
    xw,
    seg,
    rowhot,
    colhot,
    foldhot,
    y_ref,
    own32,
    partial32,
    outgoing,
    incoming,
    gsum,
    stage_a,
    stage_b,
    natural,
    tile_sem,
    z_send,
    z_recv,
    x_send,
    x_recv,
    c_send,
    c_recv,
    s_send,
    s_recv,
    p_send,
    p_recv,
    a_send,
    a_recv,
    b_send,
    b_recv,
):
    row, col = lax.axis_index("row"), lax.axis_index("col")
    core, xl, z = row % 2, (row // 2) % 2, row // 4
    low = low_half()

    def row_of(z_at, xl_at, core_at):
        return (z_at * 2 + xl_at) * 2 + core_at

    def a_peer(d):
        at = (xl * 8 + col + d) % 16
        return row_of(z, at // 8, core), at % 8

    def b_peer(d):
        at = (z * 2 + core + d) % 16
        return row_of(at // 2, xl, at % 2), col

    barrier = pltpu.get_barrier_semaphore()
    for d in range(1, 16):
        for peer in (a_peer(d), b_peer(d)):
            pl.semaphore_signal(barrier, inc=1, device_id=peer, device_id_type=pl.DeviceIdType.MESH)

    def tile_copy(t):
        return pltpu.make_async_copy(tiles_ref.at[t], tile_vm.at[t], tile_sem.at[t])

    for t in range(8):
        tile_copy(t).start()

    to_blocks(vectors_ref[...].astype(F32), own32)
    xw[row] = own32[...].astype(BF16)
    seg[pl.ds(pl.multiple_of(16 * col, 16), 16), :] = own32[...].astype(BF16)

    pl.semaphore_wait(barrier, 30)

    def remote(src, dst, send, recv, peer):
        return pltpu.make_async_remote_copy(
            src_ref=src,
            dst_ref=dst,
            send_sem=send,
            recv_sem=recv,
            device_id=peer,
            device_id_type=pl.DeviceIdType.MESH,
        )

    started = []

    def send(*args):
        copy = remote(*args)
        copy.start()
        started.append(copy)

    here = (row_of(z, xl, 1 - core), col)
    across = (row_of(z, 1 - xl, core), col)
    for d in NEAR_LAST:
        peer = (row_of((z + d) % 8, xl, core), col)
        send(xw.at[row], xw.at[row], z_send.at[d], z_recv.at[d], peer)
    send(xw.at[row], xw.at[row], x_send.at[0], x_recv.at[0], across)
    send(xw.at[row], xw.at[row], c_send.at[0], c_recv.at[0], here)
    mine = seg.at[pl.ds(pl.multiple_of(16 * col, 16), 16), :]
    for d in range(1, 8):
        send(mine, mine, s_send.at[d], s_recv.at[d], (row, (col + d) % 8))

    onehots(rows_ref, cols_ref, count_ref, rowhot, colhot, foldhot)

    for d in NEAR_FIRST:
        piece = row_of((z - d) % 8, xl, core)
        remote(xw.at[piece], xw.at[piece], z_send.at[d], z_recv.at[d], across).wait_recv()
        send(xw.at[piece], xw.at[piece], x_send.at[d], x_recv.at[d], across)
        send(xw.at[piece], xw.at[piece], c_send.at[d], c_recv.at[d], here)
    for d in (0,) + NEAR_FIRST:
        piece = row_of((z - d) % 8, 1 - xl, core)
        remote(xw.at[piece], xw.at[piece], x_send.at[d], x_recv.at[d], across).wait_recv()
        send(xw.at[piece], xw.at[piece], c_send.at[8 + d], c_recv.at[8 + d], here)
    for d in range(8):
        for half in range(2):
            piece = row_of((z - d) % 8, (xl + half) % 2, 1 - core)
            at = 8 * half + d
            remote(xw.at[piece], xw.at[piece], c_send.at[at], c_recv.at[at], here).wait_recv()

    def turn_of(t, carry):
        tile_copy(t).wait()
        products(t, colhot, xw[...].reshape(512, 512), tile_vm, y_ref)
        return carry

    lax.fori_loop(0, 8, turn_of, 0)

    for p in range(4):
        total = scattered(p, rowhot, y_ref, foldhot)
        partial32[p] = total
        outgoing[:, p] = total.astype(BF16).reshape(8, 16, 128)
    for d in range(1, 8):
        peer = (row, (col + d) % 8)
        send(outgoing.at[(col + d) % 8], incoming.at[col], p_send.at[d], p_recv.at[d], peer)

    for d in range(1, 8):
        theirs = seg.at[pl.ds(pl.multiple_of(16 * ((col - d) % 8), 16), 16), :]
        remote(theirs, theirs, s_send.at[d], s_recv.at[d], here).wait_recv()

    energies = energies_ref[...]
    turned = turn(energies)
    spread = []
    for r in range(16):
        t = r // 2
        if r % 2 == 0:
            spread.append(jnp.where(low, energies[t : t + 1], turned[t : t + 1]))
        else:
            spread.append(jnp.where(low, turned[t : t + 1], energies[t : t + 1]))
    spread = jnp.concatenate(spread, axis=0)
    vec = [own32[:, 128 * p : 128 * p + 128] for p in range(4)]
    vec_turned = [turn(v) for v in vec]
    diag = [spread * v for v in vec]

    for a in range(4):
        wide = seg[:, 128 * a : 128 * a + 128].astype(F32)
        pairs = ((wide, vec[a]), (turn(wide), vec_turned[a]))
        for b in range(4):
            for kind in range(2):
                far, near = pairs[kind]
                term = (far * partial32[b]).reshape(16, 8, 128).sum(axis=0)
                term = term + (near * diag[b]).reshape(2, 8, 128).sum(axis=0)
                gsum[pl.ds(8 * a + 2 * b + kind, 1), :] = term.sum(axis=0, keepdims=True)

    lane = iota((8, 128), 1)
    sums = gsum[...]
    lows = jnp.where(low, sums, 0.0).sum(axis=1, keepdims=True)
    highs = jnp.where(low, 0.0, sums).sum(axis=1, keepdims=True)
    packed = jnp.zeros((8, 128), F32)
    for a in range(4):
        packed = jnp.where(lane == a, lows[8 * a : 8 * a + 8], packed)
        packed = jnp.where(lane == 4 + a, highs[8 * a : 8 * a + 8], packed)

    at_a, at_b = xl * 8 + col, z * 2 + core
    stage_a[at_a] = packed
    for d in range(1, 16):
        send(stage_a.at[at_a], stage_a.at[at_a], a_send.at[d], a_recv.at[d], a_peer(d))
    for d in range(1, 16):
        theirs = stage_a.at[(at_a - d) % 16]
        remote(theirs, theirs, a_send.at[d], a_recv.at[d], here).wait_recv()
    stage_b[at_b] = stage_a[...].sum(axis=0)
    for d in range(1, 16):
        send(stage_b.at[at_b], stage_b.at[at_b], b_send.at[d], b_recv.at[d], b_peer(d))

    for d in range(1, 8):
        theirs = incoming.at[(col - d) % 8]
        remote(theirs, theirs, p_send.at[d], p_recv.at[d], here).wait_recv()
    incoming[col] = jnp.zeros((4, 16, 128), BF16)
    whole = []
    for p in range(4):
        share = partial32[p, pl.ds(pl.multiple_of(16 * col, 16), 16), :]
        for c in range(8):
            share = share + incoming[c, p].astype(F32)
        whole.append(diag[p] + share)
        from_blocks(whole[p], p, natural)
    product_ref[...] = natural[...].astype(BF16)

    for d in range(1, 16):
        theirs = stage_b.at[(at_b - d) % 16]
        remote(theirs, theirs, b_send.at[d], b_recv.at[d], here).wait_recv()
    gram = stage_b[...].sum(axis=0) / n_states
    rest = list(whole)
    for a in range(4):
        coef = jnp.where(low, gram[:, a : a + 1], gram[:, 4 + a : 5 + a])
        for b in range(4):
            rest[b] = rest[b] - coef[2 * b : 2 * b + 1] * vec[a]
            rest[b] = rest[b] - coef[2 * b + 1 : 2 * b + 2] * vec_turned[a]
    for p in range(4):
        from_blocks(rest[p], p, residual_ref)

    for copy in started:
        copy.wait_send()


def per_device(vectors, energies, tiles, tile_rows, tile_cols, tile_count):
    n_states = 32 * 8 * 1024
    stored = tiles.reshape(128, 8, 32, 128).transpose(0, 2, 1, 3).reshape(8, 4096, 128)
    vmem = pl.BlockSpec(memory_space=pltpu.VMEM)
    dma = pltpu.SemaphoreType.DMA
    return pl.pallas_call(
        lambda *refs: kernel(n_states, *refs),
        out_shape=(
            jax.ShapeDtypeStruct((8, 1024), BF16),
            jax.ShapeDtypeStruct((8, 1024), F32),
        ),
        in_specs=[
            vmem,
            vmem,
            pl.BlockSpec(memory_space=pltpu.HBM),
            vmem,
            vmem,
            pl.BlockSpec(memory_space=pltpu.SMEM),
        ],
        out_specs=(vmem, vmem),
        scratch_shapes=[
            pltpu.VMEM((8, 4096, 128), BF16),
            pltpu.VMEM((32, 16, 512), BF16),
            pltpu.VMEM((128, 512), BF16),
            pltpu.VMEM((128, 1024), BF16),
            pltpu.VMEM((8, 128, 512), BF16),
            pltpu.VMEM((4, 256, 128), BF16),
            pltpu.VMEM((16, 1024, 256), BF16),
            pltpu.VMEM((16, 512), F32),
            pltpu.VMEM((4, 128, 128), F32),
            pltpu.VMEM((8, 4, 16, 128), BF16),
            pltpu.VMEM((8, 4, 16, 128), BF16),
            pltpu.VMEM((32, 128), F32),
            pltpu.VMEM((16, 8, 128), F32),
            pltpu.VMEM((16, 8, 128), F32),
            pltpu.VMEM((8, 1024), F32),
            dma((8,)),
            dma((8,)),
            dma((8,)),
            dma((8,)),
            dma((8,)),
            dma((16,)),
            dma((16,)),
            dma((8,)),
            dma((8,)),
            dma((8,)),
            dma((8,)),
            dma((16,)),
            dma((16,)),
            dma((16,)),
            dma((16,)),
        ],
        compiler_params=pltpu.CompilerParams(
            collective_id=0, has_side_effects=True, vmem_limit_bytes=48 * 2**20
        ),
    )(
        vectors,
        energies.reshape(8, 128),
        stored,
        tile_rows.reshape(8, 128),
        tile_cols.reshape(8, 128),
        tile_count,
    )


def solution(mesh):
    in_specs = (
        P(None, ("row", "col")),
        P(("row", "col")),
        P(("row", "col"), None),
        P(("row", "col")),
        P(("row", "col")),
        P(("row", "col")),
    )
    out_specs = (P(None, ("row", "col")), P(None, ("row", "col")))
    return jax.shard_map(
        per_device, mesh=mesh, in_specs=in_specs, out_specs=out_specs, check_vma=False
    )
```

```python
import jax
import jax.numpy as jnp
from jax import lax
from jax.experimental import pallas as pl
from jax.experimental.pallas import tpu as pltpu
from jax.sharding import PartitionSpec as P

F32, BF16 = jnp.float32, jnp.bfloat16


def iota(shape, dim):
    return lax.broadcasted_iota(jnp.int32, shape, dim)


def low_half():
    return iota((1, 128), 1) < 64


def turn(value):
    return pltpu.roll(value, 64, 1)


def to_blocks(natural, out_ref):
    low = low_half()
    for t in range(8):
        part = natural[:, 128 * t : 128 * t + 128]
        turned = turn(part)
        for p in range(4):
            a, b = 2 * p, 2 * p + 1
            lanes = pl.ds(128 * p, 128)
            out_ref[pl.ds(2 * t, 1), lanes] = jnp.where(low, part[a : a + 1], turned[b : b + 1])
            out_ref[pl.ds(2 * t + 1, 1), lanes] = jnp.where(low, turned[a : a + 1], part[b : b + 1])


def from_blocks(value, p, out_ref):
    low = low_half()
    turned = turn(value)
    for t in range(8):
        a, b = 2 * t, 2 * t + 1
        lanes = pl.ds(128 * t, 128)
        out_ref[pl.ds(2 * p, 1), lanes] = jnp.where(low, value[a : a + 1], turned[b : b + 1])
        out_ref[pl.ds(2 * p + 1, 1), lanes] = jnp.where(low, turned[a : a + 1], value[b : b + 1])


def mirrored(value):
    lane = iota(value.shape, 1)
    for bit in (1, 2, 4):
        swapped = jnp.where((lane & bit) != 0, pltpu.roll(value, bit, 1), pltpu.roll(value, 128 - bit, 1))
        value = swapped
    return value


def onehots(rows_ref, cols_ref, count_ref, rowhot, colhot, foldhot):
    count = count_ref[0]
    slot = iota((8, 128), 0) * 128 + iota((8, 128), 1)
    rows = mirrored(jnp.where(slot < count, rows_ref[...], -1))
    cols = jnp.transpose(mirrored(cols_ref[...]).astype(F32))
    row_ids = iota((128, 128), 0)
    col_ids = iota((128, 512), 1).astype(F32)
    for t in range(8):
        hot = row_ids == rows[t : t + 1, :]
        rowhot[:, 128 * t : 128 * t + 128] = jnp.where(hot, 1.0, 0.0).astype(BF16)
        hot = cols[:, t : t + 1] == col_ids
        colhot[128 * t : 128 * t + 128, :] = jnp.where(hot, 1.0, 0.0).astype(BF16)
    at = iota((256, 512), 0)
    spot = 64 * (at % 8) + 2 * (at // 8)
    lane = iota((256, 512), 1)
    for jp in range(2):
        foldhot[jp] = jnp.where(lane == spot + jp, 1.0, 0.0).astype(BF16)


def products(t, x_ref, tile_ref, z_ref):
    low = low_half()
    parts = []
    for jp in range(2):
        keep = low if jp == 0 else jnp.logical_not(low)
        for k in range(8):
            value = x_ref[pl.ds(pl.multiple_of(128 * t, 128), 128), 128 * (k // 2) : 128 * (k // 2) + 128]
            if k % 2 != jp:
                value = turn(value)
            parts.append(jnp.where(keep, value, 0.0))
    away = (iota((8, 128), 1) + iota((8, 128), 0) + 1) % 8
    outs = []
    for g in range(16):
        left = jnp.concatenate([part[8 * g : 8 * g + 8] for part in parts], axis=0).astype(BF16)
        right = tile_ref[t, pl.ds(256 * g, 256), :]
        out = lax.dot_general(left, right, (((1,), (1,)), ((), ())), preferred_element_type=F32)
        merged = []
        for jp in range(2):
            for h in range(2):
                lanes = slice(128 * h, 128 * h + 128)
                both = out[64 * jp : 64 * jp + 8, lanes]
                for k in range(1, 8):
                    first = 64 * jp + 8 * k
                    moved = pltpu.roll(out[first : first + 8, lanes], k, 1)
                    both = jnp.where(away == k, moved, both)
                merged.append(pltpu.roll(both, 121, 1, stride=1, stride_axis=0))
        outs.append(merged)
        if g % 2 == 1:
            first = pl.multiple_of(128 * t + 8 * (g - 1), 16)
            for jp in range(2):
                for h in range(2):
                    pair = [o[2 * jp + h] for o in outs]
                    z_ref[jp, pl.ds(first, 16), 128 * h : 128 * h + 128] = jnp.concatenate(pair, axis=0).astype(BF16)
            outs = []


def scattered(rowhot, z_ref, foldhot):
    hots = rowhot[...]
    total = None
    for jp in range(2):
        acc = jnp.dot(hots, z_ref[jp], preferred_element_type=F32)
        upper = acc.astype(BF16)
        lower = (acc - upper.astype(F32)).astype(BF16)
        for half in (upper, lower):
            term = jnp.dot(half, foldhot[jp], preferred_element_type=F32)
            total = term if total is None else total + term
    return total


def kernel(
    n_states,
    vectors_ref,
    energies_ref,
    tiles_ref,
    rows_ref,
    cols_ref,
    count_ref,
    product_ref,
    residual_ref,
    vectors_vm,
    energies_vm,
    rows_vm,
    cols_vm,
    tile_vm,
    xw,
    seg,
    rowhot,
    colhot,
    foldhot,
    x_ref,
    z_ref,
    own32,
    partial32,
    outgoing,
    incoming,
    gsum,
    stage_a,
    stage_b,
    natural,
    in_sem,
    tile_sem,
    z_recv,
    x_recv,
    send_sem,
    recv_sem,
    known,
):
    row, col = lax.axis_index("row"), lax.axis_index("col")
    core, xl, z = row % 2, (row // 2) % 2, row // 4
    xh, y = col % 2, col // 2
    low = low_half()

    def at(z_at, x_at, core_at, y_at):
        return (z_at * 2 + x_at % 2) * 2 + core_at, y_at * 2 + x_at // 2

    x = xh * 2 + xl
    z_peer = [at((z + d) % 8, x, core, y) for d in range(8)]
    x_peer = [at(z, (x + d) % 4, core, y) for d in range(4)]
    y_peer = [at(z, x, core, (y + d) % 4) for d in range(4)]
    here = at(z, x, 1 - core, y)
    across = at(z, xh * 2 + 1 - xl, core, y)
    plane_peer = [at(z, (x + d // 4) % 4, core, (y + d % 4) % 4) for d in range(16)]
    line_peer = [at((z + d // 2) % 8, x, (core + d) % 2, y) for d in range(16)]
    mesh_ids = pl.DeviceIdType.MESH

    barrier = pltpu.get_barrier_semaphore()
    near = (z_peer[2], z_peer[6], x_peer[2], y_peer[2], z_peer[1], z_peer[7])
    near = near + (x_peer[1], x_peer[3], y_peer[1], y_peer[3], here)
    for peer in near:
        pl.semaphore_signal(barrier, inc=1, device_id=peer, device_id_type=mesh_ids)

    loads = [
        pltpu.make_async_copy(src, dst, in_sem.at[i])
        for i, (src, dst) in enumerate(
            (
                (vectors_ref, vectors_vm),
                (cols_ref, cols_vm),
                (rows_ref, rows_vm),
                (energies_ref, energies_vm),
            )
        )
    ]
    for load in loads:
        load.start()

    def tile_copy(t):
        return pltpu.make_async_copy(tiles_ref.at[t], tile_vm.at[t], tile_sem.at[t])

    for t in range(8):
        tile_copy(t).start()

    mine = seg.at[pl.ds(pl.multiple_of(16 * col, 16), 16), :]
    loads[0].wait()
    to_blocks(vectors_vm[...].astype(F32), own32)
    xw[row] = own32[...].astype(BF16)
    mine[...] = own32[...].astype(BF16)

    pl.semaphore_wait(barrier, len(near))

    def remote(src, dst, send, recv, peer):
        return pltpu.make_async_remote_copy(
            src_ref=src,
            dst_ref=dst,
            send_sem=send,
            recv_sem=recv,
            device_id=peer,
            device_id_type=mesh_ids,
        )

    def arrived(ref, recv):
        remote(ref, ref, send_sem.at[0], recv, here).wait_recv()

    def sent(ref, i):
        remote(ref, ref, send_sem.at[i], recv_sem.at[i], here).wait_send()

    def pass_on(piece, recv, peer):
        remote(xw.at[piece], xw.at[piece], send_sem.at[0], recv, peer).start()

    def to_x_and_core(piece, e):
        pass_on(piece, x_recv.at[e], across)
        pass_on(piece, recv_sem.at[0], here)

    for d in (2, 6, 1, 7):
        pass_on(row, z_recv.at[8 - d], z_peer[d])
    to_x_and_core(row, 0)
    for d in range(1, 4):
        pl.semaphore_signal(known, inc=1, device_id=y_peer[d], device_id_type=mesh_ids)

    for load in loads[1:]:
        load.wait()
    onehots(rows_vm, cols_vm, count_ref, rowhot, colhot, foldhot)

    further = {1: (6, 3), 7: (2, 5), 2: (6, 4)}

    def from_z(e):
        piece = z_peer[e][0]
        arrived(xw.at[piece], z_recv.at[e])
        if e in further:
            d, there = further[e]
            pass_on(piece, z_recv.at[there], z_peer[d])
        to_x_and_core(piece, e)

    def from_x(e):
        piece = at((z + e) % 8, xh * 2 + 1 - xl, core, y)[0]
        arrived(xw.at[piece], x_recv.at[e])
        pass_on(piece, recv_sem.at[0], here)

    for e in (1, 7, 2, 6):
        from_z(e)
    for e in (0, 1, 7):
        from_x(e)
    for e in (3, 5, 4):
        from_z(e)
    for e in (2, 6, 3, 5, 4):
        from_x(e)
    pl.semaphore_wait(known, 3)
    for d in range(1, 8):
        remote(mine, mine, send_sem.at[1], recv_sem.at[1], (row, (col + d) % 8)).start()
    arrived(xw.at[pl.ds(0, 16)], recv_sem.at[0])

    x_ref[...] = jnp.dot(colhot[...], xw[...].reshape(512, 512), preferred_element_type=F32)

    def turn_of(t, carry):
        tile_copy(t).wait()
        products(t, x_ref, tile_vm, z_ref)
        return carry

    lax.fori_loop(0, 8, turn_of, 0)

    partial32[...] = scattered(rowhot, z_ref, foldhot)
    for p in range(4):
        outgoing[:, p] = partial32[:, 128 * p : 128 * p + 128].astype(BF16).reshape(8, 16, 128)
    arrived(seg.at[pl.ds(0, 112), :], recv_sem.at[1])
    for d in range(1, 8):
        to = (col + d) % 8
        remote(outgoing.at[to], incoming.at[col], send_sem.at[2], recv_sem.at[2], (row, to)).start()

    energies = energies_vm[...]
    turned = turn(energies)
    spread = []
    for r in range(16):
        t = r // 2
        if r % 2 == 0:
            spread.append(jnp.where(low, energies[t : t + 1], turned[t : t + 1]))
        else:
            spread.append(jnp.where(low, turned[t : t + 1], energies[t : t + 1]))
    spread = jnp.concatenate(spread, axis=0)
    vec = [own32[:, 128 * p : 128 * p + 128] for p in range(4)]
    vec_turned = [turn(v) for v in vec]
    diag = [spread * v for v in vec]

    for a in range(4):
        wide = seg[:, 128 * a : 128 * a + 128].astype(F32)
        pairs = ((wide, vec[a]), (turn(wide), vec_turned[a]))
        for b in range(4):
            for kind in range(2):
                far, close = pairs[kind]
                term = (far * partial32[:, 128 * b : 128 * b + 128]).reshape(16, 8, 128).sum(axis=0)
                term = term + (close * diag[b]).reshape(2, 8, 128).sum(axis=0)
                gsum[pl.ds(8 * a + 2 * b + kind, 1), :] = term.sum(axis=0, keepdims=True)

    lane = iota((8, 128), 1)
    sums = gsum[...]
    lows = jnp.where(low, sums, 0.0).sum(axis=1, keepdims=True)
    highs = jnp.where(low, 0.0, sums).sum(axis=1, keepdims=True)
    packed = jnp.zeros((8, 128), F32)
    for a in range(4):
        packed = jnp.where(lane == a, lows[8 * a : 8 * a + 8], packed)
        packed = jnp.where(lane == 4 + a, highs[8 * a : 8 * a + 8], packed)

    at_a, at_b = x * 4 + y, z * 2 + core
    stage_a[at_a] = packed
    far_first = (10, 11, 9, 14, 6, 2, 8, 15, 13, 7, 5, 3, 1, 12, 4)
    for d in far_first:
        remote(stage_a.at[at_a], stage_a.at[at_a], send_sem.at[3], recv_sem.at[3], plane_peer[d]).start()
    arrived(stage_a.at[pl.ds(0, 15)], recv_sem.at[3])
    stage_b[at_b] = stage_a[...].sum(axis=0)
    far_first = (8, 9, 6, 7, 10, 11, 4, 5, 12, 13, 2, 3, 14, 15, 1)
    for d in far_first:
        remote(stage_b.at[at_b], stage_b.at[at_b], send_sem.at[4], recv_sem.at[4], line_peer[d]).start()

    sent(xw.at[pl.ds(0, 31)], 0)
    sent(seg.at[pl.ds(0, 112), :], 1)
    sent(outgoing.at[pl.ds(0, 7)], 2)
    sent(stage_a.at[pl.ds(0, 15)], 3)

    arrived(incoming.at[pl.ds(0, 7)], recv_sem.at[2])
    incoming[col] = jnp.zeros((4, 16, 128), BF16)
    whole = []
    own_rows = pl.ds(pl.multiple_of(16 * col, 16), 16)
    for p in range(4):
        share = partial32[own_rows, 128 * p : 128 * p + 128]
        for c in range(8):
            share = share + incoming[c, p].astype(F32)
        whole.append(diag[p] + share)
        from_blocks(whole[p], p, natural)
    product_ref[...] = natural[...].astype(BF16)

    arrived(stage_b.at[pl.ds(0, 15)], recv_sem.at[4])
    gram = stage_b[...].sum(axis=0) / n_states
    rest = list(whole)
    for a in range(4):
        coef = jnp.where(low, gram[:, a : a + 1], gram[:, 4 + a : 5 + a])
        for b in range(4):
            rest[b] = rest[b] - coef[2 * b : 2 * b + 1] * vec[a]
            rest[b] = rest[b] - coef[2 * b + 1 : 2 * b + 2] * vec_turned[a]
    for p in range(4):
        from_blocks(rest[p], p, residual_ref)
    sent(stage_b.at[pl.ds(0, 15)], 4)


def per_device(vectors, energies, tiles, tile_rows, tile_cols, tile_count):
    n_states = 32 * 8 * 1024
    stored = tiles.reshape(128, 8, 32, 128).transpose(0, 2, 1, 3).reshape(8, 4096, 128)
    vmem = pl.BlockSpec(memory_space=pltpu.VMEM)
    hbm = pl.BlockSpec(memory_space=pltpu.HBM)
    dma = pltpu.SemaphoreType.DMA
    return pl.pallas_call(
        lambda *refs: kernel(n_states, *refs),
        out_shape=(
            jax.ShapeDtypeStruct((8, 1024), BF16),
            jax.ShapeDtypeStruct((8, 1024), F32),
        ),
        in_specs=[hbm, hbm, hbm, hbm, hbm, pl.BlockSpec(memory_space=pltpu.SMEM)],
        out_specs=(vmem, vmem),
        scratch_shapes=[
            pltpu.VMEM((8, 1024), BF16),
            pltpu.VMEM((8, 128), F32),
            pltpu.VMEM((8, 128), jnp.int32),
            pltpu.VMEM((8, 128), jnp.int32),
            pltpu.VMEM((8, 4096, 128), BF16),
            pltpu.VMEM((32, 16, 512), BF16),
            pltpu.VMEM((128, 512), BF16),
            pltpu.VMEM((128, 1024), BF16),
            pltpu.VMEM((1024, 512), BF16),
            pltpu.VMEM((2, 256, 512), BF16),
            pltpu.VMEM((1024, 512), F32),
            pltpu.VMEM((2, 1024, 256), BF16),
            pltpu.VMEM((16, 512), F32),
            pltpu.VMEM((128, 512), F32),
            pltpu.VMEM((8, 4, 16, 128), BF16),
            pltpu.VMEM((8, 4, 16, 128), BF16),
            pltpu.VMEM((32, 128), F32),
            pltpu.VMEM((16, 8, 128), F32),
            pltpu.VMEM((16, 8, 128), F32),
            pltpu.VMEM((8, 1024), F32),
            dma((4,)),
            dma((8,)),
            dma((8,)),
            dma((8,)),
            dma((5,)),
            dma((5,)),
            pltpu.SemaphoreType.REGULAR,
        ],
        compiler_params=pltpu.CompilerParams(
            collective_id=0, has_side_effects=True, vmem_limit_bytes=48 * 2**20
        ),
    )(
        vectors,
        energies.reshape(8, 128),
        stored,
        tile_rows.reshape(8, 128),
        tile_cols.reshape(8, 128),
        tile_count,
    )


def solution(mesh):
    in_specs = (
        P(None, ("row", "col")),
        P(("row", "col")),
        P(("row", "col"), None),
        P(("row", "col")),
        P(("row", "col")),
        P(("row", "col")),
    )
    out_specs = (P(None, ("row", "col")), P(None, ("row", "col")))
    return jax.shard_map(
        per_device, mesh=mesh, in_specs=in_specs, out_specs=out_specs, check_vma=False
    )
```

```python
import jax
import jax.numpy as jnp
from jax import lax
from jax.experimental import pallas as pl
from jax.experimental.pallas import tpu as pltpu
from jax.sharding import PartitionSpec as P

F32, BF16 = jnp.float32, jnp.bfloat16


def iota(shape, dim):
    return lax.broadcasted_iota(jnp.int32, shape, dim)


def low_half():
    return iota((1, 128), 1) < 64


def turn(value):
    return pltpu.roll(value, 64, 1)


def to_blocks(natural, out_ref):
    low = low_half()
    for t in range(8):
        part = natural[:, 128 * t : 128 * t + 128]
        turned = turn(part)
        for p in range(4):
            a, b = 2 * p, 2 * p + 1
            lanes = pl.ds(128 * p, 128)
            out_ref[pl.ds(2 * t, 1), lanes] = jnp.where(low, part[a : a + 1], turned[b : b + 1])
            out_ref[pl.ds(2 * t + 1, 1), lanes] = jnp.where(low, turned[a : a + 1], part[b : b + 1])


def from_blocks(value, p, out_ref):
    low = low_half()
    turned = turn(value)
    for t in range(8):
        a, b = 2 * t, 2 * t + 1
        lanes = pl.ds(128 * t, 128)
        out_ref[pl.ds(2 * p, 1), lanes] = jnp.where(low, value[a : a + 1], turned[b : b + 1])
        out_ref[pl.ds(2 * p + 1, 1), lanes] = jnp.where(low, turned[a : a + 1], value[b : b + 1])


def mirrored(value):
    lane = iota(value.shape, 1)
    for bit in (1, 2, 4):
        swapped = jnp.where((lane & bit) != 0, pltpu.roll(value, bit, 1), pltpu.roll(value, 128 - bit, 1))
        value = swapped
    return value


def onehots(rows_ref, cols_ref, count_ref, rowhot, colhot, foldhot):
    count = count_ref[0]
    slot = iota((8, 128), 0) * 128 + iota((8, 128), 1)
    rows = mirrored(jnp.where(slot < count, rows_ref[...], -1))
    cols = jnp.transpose(mirrored(cols_ref[...]).astype(F32))
    row_ids = iota((128, 128), 0)
    col_ids = iota((128, 512), 1).astype(F32)
    for t in range(8):
        hot = row_ids == rows[t : t + 1, :]
        rowhot[:, 128 * t : 128 * t + 128] = jnp.where(hot, 1.0, 0.0).astype(BF16)
        hot = cols[:, t : t + 1] == col_ids
        colhot[128 * t : 128 * t + 128, :] = jnp.where(hot, 1.0, 0.0).astype(BF16)
    at = iota((256, 512), 0)
    spot = 64 * (at % 8) + 2 * (at // 8)
    lane = iota((256, 512), 1)
    for jp in range(2):
        foldhot[jp] = jnp.where(lane == spot + jp, 1.0, 0.0).astype(BF16)


def products(t, x_ref, tile_ref, z_ref):
    low = low_half()
    parts = []
    for jp in range(2):
        keep = low if jp == 0 else jnp.logical_not(low)
        for k in range(8):
            value = x_ref[pl.ds(128 * t, 128), 128 * (k // 2) : 128 * (k // 2) + 128]
            if k % 2 != jp:
                value = turn(value)
            parts.append(jnp.where(keep, value, 0.0))
    away = (iota((8, 128), 1) + iota((8, 128), 0) + 1) % 8
    outs = []
    for g in range(16):
        left = jnp.concatenate([part[8 * g : 8 * g + 8] for part in parts], axis=0).astype(BF16)
        right = tile_ref[t, pl.ds(256 * g, 256), :]
        out = lax.dot_general(left, right, (((1,), (1,)), ((), ())), preferred_element_type=F32)
        merged = []
        for jp in range(2):
            for h in range(2):
                lanes = slice(128 * h, 128 * h + 128)
                both = out[64 * jp : 64 * jp + 8, lanes]
                for k in range(1, 8):
                    first = 64 * jp + 8 * k
                    moved = pltpu.roll(out[first : first + 8, lanes], k, 1)
                    both = jnp.where(away == k, moved, both)
                merged.append(pltpu.roll(both, 121, 1, stride=1, stride_axis=0))
        outs.append(merged)
        if g % 2 == 1:
            first = 128 * t + 8 * (g - 1)
            for jp in range(2):
                for h in range(2):
                    pair = [o[2 * jp + h] for o in outs]
                    z_ref[jp, pl.ds(first, 16), 128 * h : 128 * h + 128] = jnp.concatenate(pair, axis=0).astype(BF16)
            outs = []


def in_two(value):
    upper = value.astype(BF16)
    return upper, (value - upper.astype(F32)).astype(BF16)


def group_sum(value):
    for shift in (64, 32, 16, 8):
        value = value + pltpu.roll(value, shift, 1)
    return value


def kernel(
    n_states,
    vectors_ref,
    energies_ref,
    tiles_ref,
    rows_ref,
    cols_ref,
    count_ref,
    product_ref,
    residual_ref,
    vectors_vm,
    energies_vm,
    rows_vm,
    cols_vm,
    tile_vm,
    xw,
    seg,
    rowhot,
    colhot,
    foldhot,
    x_ref,
    z_ref,
    own32,
    partial32,
    outgoing,
    incoming,
    gsum,
    seg_t,
    shares,
    stage_a,
    stage_b,
    natural,
    in_sem,
    tile_sem,
    z_recv,
    x_recv,
    send_sem,
    recv_sem,
    known,
):
    row, col = lax.axis_index("row"), lax.axis_index("col")
    core, xl, z = row % 2, (row // 2) % 2, row // 4
    xh, y = col % 2, col // 2
    low = low_half()

    def at(z_at, x_at, core_at, y_at):
        return (z_at * 2 + x_at % 2) * 2 + core_at, y_at * 2 + x_at // 2

    x = xh * 2 + xl
    z_peer = [at((z + d) % 8, x, core, y) for d in range(8)]
    x_peer = [at(z, (x + d) % 4, core, y) for d in range(4)]
    y_peer = [at(z, x, core, (y + d) % 4) for d in range(4)]
    here = at(z, x, 1 - core, y)
    across = at(z, xh * 2 + 1 - xl, core, y)
    plane_peer = [at(z, (x + d // 4) % 4, core, (y + d % 4) % 4) for d in range(16)]
    line_peer = [at((z + d // 2) % 8, x, (core + d) % 2, y) for d in range(16)]
    mesh_ids = pl.DeviceIdType.MESH

    barrier = pltpu.get_barrier_semaphore()
    near = (z_peer[2], z_peer[6], x_peer[2], y_peer[2], z_peer[1], z_peer[7])
    near = near + (x_peer[1], x_peer[3], y_peer[1], y_peer[3], here)

    loads = [
        pltpu.make_async_copy(src, dst, in_sem.at[i])
        for i, (src, dst) in enumerate(
            (
                (vectors_ref, vectors_vm),
                (cols_ref, cols_vm),
                (rows_ref, rows_vm),
                (energies_ref, energies_vm),
            )
        )
    ]
    loads[0].start()
    for peer in near:
        pl.semaphore_signal(barrier, inc=1, device_id=peer, device_id_type=mesh_ids)

    def tile_copy(t):
        return pltpu.make_async_copy(tiles_ref.at[t], tile_vm.at[t], tile_sem.at[t])

    mine = seg.at[pl.ds(pl.multiple_of(16 * col, 16), 16), :]
    loads[0].wait()
    own = vectors_vm[...].astype(F32)
    to_blocks(own, own32)
    xw[row] = own32[...].astype(BF16)
    mine[...] = own32[...].astype(BF16)

    pl.semaphore_wait(barrier, len(near))

    def remote(src, dst, send, recv, peer):
        return pltpu.make_async_remote_copy(
            src_ref=src,
            dst_ref=dst,
            send_sem=send,
            recv_sem=recv,
            device_id=peer,
            device_id_type=mesh_ids,
        )

    def arrived(ref, recv):
        remote(ref, ref, send_sem.at[0], recv, here).wait_recv()

    def sent(ref, i):
        remote(ref, ref, send_sem.at[i], recv_sem.at[i], here).wait_send()

    def pass_on(piece, recv, peer):
        remote(xw.at[piece], xw.at[piece], send_sem.at[0], recv, peer).start()

    def to_x_and_core(piece, e):
        pass_on(piece, x_recv.at[e], across)
        pass_on(piece, recv_sem.at[0], here)

    for d in (2, 6, 1, 7):
        pass_on(row, z_recv.at[8 - d], z_peer[d])
    to_x_and_core(row, 0)

    def share(ref, recv, peer):
        remote(ref, ref, send_sem.at[1], recv, peer).start()

    share(mine, x_recv.at[8], x_peer[2])
    for d in (2, 1, 3):
        pl.semaphore_signal(known, inc=1, device_id=y_peer[d], device_id_type=mesh_ids)
        share(mine, recv_sem.at[1], y_peer[d])

    for load in loads[1:]:
        load.start()
    for t in range(8):
        tile_copy(t).start()
    for load in loads[1:]:
        load.wait()
    onehots(rows_vm, cols_vm, count_ref, rowhot, colhot, foldhot)
    energies = energies_vm[...]
    diag = [own[:, 128 * t : 128 * t + 128] * energies[t : t + 1] for t in range(8)]
    diag = jnp.concatenate(diag, axis=1)
    natural[...] = diag
    upper = diag.astype(BF16).astype(F32)
    halves = jnp.concatenate([upper, diag - upper, jnp.zeros((112, 1024), F32)], axis=0)
    gsum[...] = lax.dot_general(
        vectors_vm[...], halves.astype(BF16), (((1,), (1,)), ((), ())), preferred_element_type=F32
    )

    further = {1: (6, 3), 7: (2, 5), 2: (6, 4)}

    def from_z(e):
        piece = z_peer[e][0]
        arrived(xw.at[piece], z_recv.at[e])
        if e in further:
            d, there = further[e]
            pass_on(piece, z_recv.at[there], z_peer[d])
        to_x_and_core(piece, e)

    def from_x(e):
        piece = at((z + e) % 8, xh * 2 + 1 - xl, core, y)[0]
        arrived(xw.at[piece], x_recv.at[e])
        pass_on(piece, recv_sem.at[0], here)

    for e in (1, 7, 2, 6):
        from_z(e)
    theirs = seg.at[pl.ds(pl.multiple_of(16 * (2 * y + 1 - xh), 16), 16), :]
    arrived(theirs, x_recv.at[8])
    for d in (2, 1, 3):
        share(theirs, recv_sem.at[1], y_peer[d])
    for e in (0, 1, 7):
        from_x(e)
    for e in (3, 5, 4):
        from_z(e)
    for e in (2, 6, 3, 5, 4):
        from_x(e)
    pl.semaphore_wait(known, 3)
    for t in range(8):
        tile_copy(t).wait()
    arrived(seg.at[pl.ds(0, 96), :], recv_sem.at[1])
    for jp in range(2):
        turned = lax.dot_general(
            foldhot[jp], seg[...], (((1,), (1,)), ((), ())), preferred_element_type=F32
        )
        seg_t[jp] = turned.astype(BF16)
    arrived(xw.at[pl.ds(0, 16)], recv_sem.at[0])

    x_ref[...] = jnp.dot(colhot[...], xw[...].reshape(512, 512), preferred_element_type=F32)
    for t in range(8):
        products(t, x_ref, tile_vm, z_ref)

    sums = [jnp.dot(rowhot[...], z_ref[jp], preferred_element_type=F32) for jp in range(2)]
    cross = jnp.zeros((256, 256), F32)
    for jp in range(2):
        for half in in_two(sums[jp]):
            cross = cross + jnp.dot(seg_t[jp], half, preferred_element_type=F32)
    group = iota((8, 128), 1) // 8
    packed = gsum[...]
    for c in range(32):
        block = cross[8 * c : 8 * c + 8, 128 * (c // 16) : 128 * (c // 16) + 128]
        packed = packed + jnp.where(group == c % 16, block, 0.0)
    packed = group_sum(packed)

    at_a, at_b = x * 4 + y, z * 2 + core
    stage_a[at_a] = packed
    far_first = (10, 11, 9, 14, 6, 2, 8, 15, 13, 7, 5, 3, 1, 12, 4)
    for d in far_first:
        remote(stage_a.at[at_a], stage_a.at[at_a], send_sem.at[3], recv_sem.at[3], plane_peer[d]).start()

    total = None
    for jp in range(2):
        for half in in_two(sums[jp]):
            term = jnp.dot(half, foldhot[jp], preferred_element_type=F32)
            total = term if total is None else total + term
    partial32[...] = total
    for p in range(4):
        outgoing[:, p] = total[:, 128 * p : 128 * p + 128].astype(BF16).reshape(8, 16, 128)
    for d in range(1, 8):
        to = (col + d) % 8
        remote(outgoing.at[to], incoming.at[col], send_sem.at[2], recv_sem.at[2], (row, to)).start()

    arrived(stage_a.at[pl.ds(0, 15)], recv_sem.at[3])
    stage_b[at_b] = stage_a[...].sum(axis=0)
    far_first = (8, 9, 6, 7, 10, 11, 4, 5, 12, 13, 2, 3, 14, 15, 1)
    for d in far_first:
        remote(stage_b.at[at_b], stage_b.at[at_b], send_sem.at[4], recv_sem.at[4], line_peer[d]).start()

    sent(xw.at[pl.ds(0, 31)], 0)
    sent(seg.at[pl.ds(0, 112), :], 1)
    sent(outgoing.at[pl.ds(0, 7)], 2)
    sent(stage_a.at[pl.ds(0, 15)], 3)

    arrived(incoming.at[pl.ds(0, 7)], recv_sem.at[2])
    incoming[col] = jnp.zeros((4, 16, 128), BF16)
    own_rows = pl.ds(pl.multiple_of(16 * col, 16), 16)
    for p in range(4):
        share_p = partial32[own_rows, 128 * p : 128 * p + 128]
        for c in range(8):
            share_p = share_p + incoming[c, p].astype(F32)
        from_blocks(share_p, p, shares)
    whole = natural[...] + shares[...]
    product_ref[...] = whole.astype(BF16)

    arrived(stage_b.at[pl.ds(0, 15)], recv_sem.at[4])
    gram = stage_b[...].sum(axis=0) / n_states
    same = iota((8, 128), 0) == iota((8, 128), 1)
    rest = whole
    for a in range(8):
        coef = jnp.where(same, gram[a : a + 1], 0.0).sum(axis=1, keepdims=True)
        rest = rest - coef * own[a : a + 1]
    residual_ref[...] = rest
    sent(stage_b.at[pl.ds(0, 15)], 4)


def per_device(vectors, energies, tiles, tile_rows, tile_cols, tile_count):
    n_states = 32 * 8 * 1024
    stored = tiles.reshape(128, 8, 32, 128).transpose(0, 2, 1, 3).reshape(8, 4096, 128)
    vmem = pl.BlockSpec(memory_space=pltpu.VMEM)
    hbm = pl.BlockSpec(memory_space=pltpu.HBM)
    dma = pltpu.SemaphoreType.DMA
    return pl.pallas_call(
        lambda *refs: kernel(n_states, *refs),
        out_shape=(
            jax.ShapeDtypeStruct((8, 1024), BF16),
            jax.ShapeDtypeStruct((8, 1024), F32),
        ),
        in_specs=[hbm, hbm, hbm, hbm, hbm, pl.BlockSpec(memory_space=pltpu.SMEM)],
        out_specs=(vmem, vmem),
        scratch_shapes=[
            pltpu.VMEM((8, 1024), BF16),
            pltpu.VMEM((8, 128), F32),
            pltpu.VMEM((8, 128), jnp.int32),
            pltpu.VMEM((8, 128), jnp.int32),
            pltpu.VMEM((8, 4096, 128), BF16),
            pltpu.VMEM((32, 16, 512), BF16),
            pltpu.VMEM((128, 512), BF16),
            pltpu.VMEM((128, 1024), BF16),
            pltpu.VMEM((1024, 512), BF16),
            pltpu.VMEM((2, 256, 512), BF16),
            pltpu.VMEM((1024, 512), F32),
            pltpu.VMEM((2, 1024, 256), BF16),
            pltpu.VMEM((16, 512), F32),
            pltpu.VMEM((128, 512), F32),
            pltpu.VMEM((8, 4, 16, 128), BF16),
            pltpu.VMEM((8, 4, 16, 128), BF16),
            pltpu.VMEM((8, 128), F32),
            pltpu.VMEM((2, 256, 128), BF16),
            pltpu.VMEM((8, 1024), F32),
            pltpu.VMEM((16, 8, 128), F32),
            pltpu.VMEM((16, 8, 128), F32),
            pltpu.VMEM((8, 1024), F32),
            dma((4,)),
            dma((8,)),
            dma((8,)),
            dma((9,)),
            dma((5,)),
            dma((5,)),
            pltpu.SemaphoreType.REGULAR,
        ],
        compiler_params=pltpu.CompilerParams(
            collective_id=0, has_side_effects=True, vmem_limit_bytes=67_043_328
        ),
    )(
        vectors,
        energies.reshape(8, 128),
        stored,
        tile_rows.reshape(8, 128),
        tile_cols.reshape(8, 128),
        tile_count,
    )


def solution(mesh):
    in_specs = (
        P(None, ("row", "col")),
        P(("row", "col")),
        P(("row", "col"), None),
        P(("row", "col")),
        P(("row", "col")),
        P(("row", "col")),
    )
    out_specs = (P(None, ("row", "col")), P(None, ("row", "col")))
    return jax.shard_map(
        per_device, mesh=mesh, in_specs=in_specs, out_specs=out_specs, check_vma=False
    )
```

```python
import jax
import jax.numpy as jnp
from jax import lax
from jax.experimental import pallas as pl
from jax.experimental.pallas import tpu as pltpu
from jax.sharding import PartitionSpec as P

F32, BF16 = jnp.float32, jnp.bfloat16


def iota(shape, dim):
    return lax.broadcasted_iota(jnp.int32, shape, dim)


def low_half():
    return iota((1, 128), 1) < 64


def turn(value):
    return pltpu.roll(value, 64, 1)


def to_blocks(natural, out_ref):
    low = low_half()
    for t in range(8):
        part = natural[:, 128 * t : 128 * t + 128]
        turned = turn(part)
        for p in range(4):
            a, b = 2 * p, 2 * p + 1
            lanes = pl.ds(128 * p, 128)
            out_ref[pl.ds(2 * t, 1), lanes] = jnp.where(low, part[a : a + 1], turned[b : b + 1])
            out_ref[pl.ds(2 * t + 1, 1), lanes] = jnp.where(low, turned[a : a + 1], part[b : b + 1])


def from_blocks(value, p, out_ref):
    low = low_half()
    turned = turn(value)
    for t in range(8):
        a, b = 2 * t, 2 * t + 1
        lanes = pl.ds(128 * t, 128)
        out_ref[pl.ds(2 * p, 1), lanes] = jnp.where(low, value[a : a + 1], turned[b : b + 1])
        out_ref[pl.ds(2 * p + 1, 1), lanes] = jnp.where(low, turned[a : a + 1], value[b : b + 1])


def mirrored(value):
    lane = iota(value.shape, 1)
    for bit in (1, 2, 4):
        swapped = jnp.where((lane & bit) != 0, pltpu.roll(value, bit, 1), pltpu.roll(value, 128 - bit, 1))
        value = swapped
    return value


def onehots(rows_ref, cols_ref, count_ref, rowhot, colhot, foldhot):
    count = count_ref[0]
    slot = iota((8, 128), 0) * 128 + iota((8, 128), 1)
    rows = mirrored(jnp.where(slot < count, rows_ref[...], -1))
    cols = jnp.transpose(mirrored(cols_ref[...]).astype(F32))
    row_ids = iota((128, 128), 0)
    col_ids = iota((128, 512), 1).astype(F32)
    for t in range(8):
        hot = row_ids == rows[t : t + 1, :]
        rowhot[:, 128 * t : 128 * t + 128] = jnp.where(hot, 1.0, 0.0).astype(BF16)
        hot = cols[:, t : t + 1] == col_ids
        colhot[128 * t : 128 * t + 128, :] = jnp.where(hot, 1.0, 0.0).astype(BF16)
    at = iota((256, 512), 0)
    spot = 64 * (at % 8) + 2 * (at // 8)
    lane = iota((256, 512), 1)
    for jp in range(2):
        foldhot[jp] = jnp.where(lane == spot + jp, 1.0, 0.0).astype(BF16)


def products(t, x_ref, tile_ref, z_ref):
    low = low_half()
    parts = []
    for jp in range(2):
        keep = low if jp == 0 else jnp.logical_not(low)
        for k in range(8):
            value = x_ref[pl.ds(128 * t, 128), 128 * (k // 2) : 128 * (k // 2) + 128]
            if k % 2 != jp:
                value = turn(value)
            parts.append(jnp.where(keep, value, 0.0))
    away = (iota((8, 128), 1) + iota((8, 128), 0) + 1) % 8
    outs = []
    for g in range(16):
        left = jnp.concatenate([part[8 * g : 8 * g + 8] for part in parts], axis=0).astype(BF16)
        right = tile_ref[t, pl.ds(256 * g, 256), :]
        out = lax.dot_general(left, right, (((1,), (1,)), ((), ())), preferred_element_type=F32)
        merged = []
        for jp in range(2):
            for h in range(2):
                lanes = slice(128 * h, 128 * h + 128)
                both = out[64 * jp : 64 * jp + 8, lanes]
                for k in range(1, 8):
                    first = 64 * jp + 8 * k
                    moved = pltpu.roll(out[first : first + 8, lanes], k, 1)
                    both = jnp.where(away == k, moved, both)
                merged.append(pltpu.roll(both, 121, 1, stride=1, stride_axis=0))
        outs.append(merged)
        if g % 2 == 1:
            first = 128 * t + 8 * (g - 1)
            for jp in range(2):
                for h in range(2):
                    pair = [o[2 * jp + h] for o in outs]
                    z_ref[jp, pl.ds(first, 16), 128 * h : 128 * h + 128] = jnp.concatenate(pair, axis=0).astype(BF16)
            outs = []


def in_two(value):
    upper = value.astype(BF16)
    return upper, (value - upper.astype(F32)).astype(BF16)


def group_sum(value):
    for shift in (64, 32, 16, 8):
        value = value + pltpu.roll(value, shift, 1)
    return value


def kernel(
    n_states,
    vectors_ref,
    energies_ref,
    tiles_ref,
    rows_ref,
    cols_ref,
    count_ref,
    whole_ref,
    along_ref,
    vectors_vm,
    energies_vm,
    rows_vm,
    cols_vm,
    tile_vm,
    xw,
    seg,
    rowhot,
    colhot,
    foldhot,
    x_ref,
    z_ref,
    own32,
    partial32,
    outgoing,
    incoming,
    gsum,
    seg_t,
    shares,
    stage_a,
    stage_b,
    natural,
    in_sem,
    tile_sem,
    z_recv,
    x_recv,
    send_sem,
    recv_sem,
    known,
):
    row, col = lax.axis_index("row"), lax.axis_index("col")
    core, xl, z = row % 2, (row // 2) % 2, row // 4
    xh, y = col % 2, col // 2
    low = low_half()

    def at(z_at, x_at, core_at, y_at):
        return (z_at * 2 + x_at % 2) * 2 + core_at, y_at * 2 + x_at // 2

    x = xh * 2 + xl
    z_peer = [at((z + d) % 8, x, core, y) for d in range(8)]
    x_peer = [at(z, (x + d) % 4, core, y) for d in range(4)]
    y_peer = [at(z, x, core, (y + d) % 4) for d in range(4)]
    here = at(z, x, 1 - core, y)
    across = at(z, xh * 2 + 1 - xl, core, y)
    plane_peer = [at(z, (x + d // 4) % 4, core, (y + d % 4) % 4) for d in range(16)]
    line_peer = [at((z + d // 2) % 8, x, (core + d) % 2, y) for d in range(16)]
    mesh_ids = pl.DeviceIdType.MESH

    barrier = pltpu.get_barrier_semaphore()
    near = (z_peer[2], z_peer[6], x_peer[2], y_peer[2], z_peer[1], z_peer[7])
    near = near + (x_peer[1], x_peer[3], y_peer[1], y_peer[3], here)

    loads = [
        pltpu.make_async_copy(src, dst, in_sem.at[i])
        for i, (src, dst) in enumerate(
            (
                (vectors_ref, vectors_vm),
                (cols_ref, cols_vm),
                (rows_ref, rows_vm),
                (energies_ref, energies_vm),
            )
        )
    ]
    loads[0].start()
    for peer in near:
        pl.semaphore_signal(barrier, inc=1, device_id=peer, device_id_type=mesh_ids)

    def tile_copy(t):
        return pltpu.make_async_copy(tiles_ref.at[t], tile_vm.at[t], tile_sem.at[t])

    mine = seg.at[pl.ds(pl.multiple_of(16 * col, 16), 16), :]
    loads[0].wait()
    own = vectors_vm[...].astype(F32)
    to_blocks(own, own32)
    xw[row] = own32[...].astype(BF16)
    mine[...] = own32[...].astype(BF16)

    pl.semaphore_wait(barrier, len(near))

    def remote(src, dst, send, recv, peer):
        return pltpu.make_async_remote_copy(
            src_ref=src,
            dst_ref=dst,
            send_sem=send,
            recv_sem=recv,
            device_id=peer,
            device_id_type=mesh_ids,
        )

    def arrived(ref, recv):
        remote(ref, ref, send_sem.at[0], recv, here).wait_recv()

    def sent(ref, i):
        remote(ref, ref, send_sem.at[i], recv_sem.at[i], here).wait_send()

    def pass_on(piece, recv, peer):
        remote(xw.at[piece], xw.at[piece], send_sem.at[0], recv, peer).start()

    def to_x_and_core(piece, e):
        pass_on(piece, x_recv.at[e], across)
        pass_on(piece, recv_sem.at[0], here)

    for d in (2, 6, 1, 7):
        pass_on(row, z_recv.at[8 - d], z_peer[d])
    to_x_and_core(row, 0)

    def share(ref, recv, peer):
        remote(ref, ref, send_sem.at[1], recv, peer).start()

    share(mine, x_recv.at[8], x_peer[2])
    for d in (2, 1, 3):
        pl.semaphore_signal(known, inc=1, device_id=y_peer[d], device_id_type=mesh_ids)
        share(mine, recv_sem.at[1], y_peer[d])

    for load in loads[1:]:
        load.start()
    for t in range(8):
        tile_copy(t).start()
    for load in loads[1:]:
        load.wait()
    onehots(rows_vm, cols_vm, count_ref, rowhot, colhot, foldhot)
    energies = energies_vm[...]
    diag = [own[:, 128 * t : 128 * t + 128] * energies[t : t + 1] for t in range(8)]
    diag = jnp.concatenate(diag, axis=1)
    natural[...] = diag
    upper = diag.astype(BF16).astype(F32)
    halves = jnp.concatenate([upper, diag - upper, jnp.zeros((112, 1024), F32)], axis=0)
    gsum[...] = lax.dot_general(
        vectors_vm[...], halves.astype(BF16), (((1,), (1,)), ((), ())), preferred_element_type=F32
    )

    further = {1: (6, 3), 7: (2, 5), 2: (6, 4)}

    def from_z(e):
        piece = z_peer[e][0]
        arrived(xw.at[piece], z_recv.at[e])
        if e in further:
            d, there = further[e]
            pass_on(piece, z_recv.at[there], z_peer[d])
        to_x_and_core(piece, e)

    def from_x(e):
        piece = at((z + e) % 8, xh * 2 + 1 - xl, core, y)[0]
        arrived(xw.at[piece], x_recv.at[e])
        pass_on(piece, recv_sem.at[0], here)

    for e in (1, 7, 2, 6):
        from_z(e)
    theirs = seg.at[pl.ds(pl.multiple_of(16 * (2 * y + 1 - xh), 16), 16), :]
    arrived(theirs, x_recv.at[8])
    for d in (2, 1, 3):
        share(theirs, recv_sem.at[1], y_peer[d])
    for e in (0, 1, 7):
        from_x(e)
    for e in (3, 5, 4):
        from_z(e)
    for e in (2, 6, 3, 5, 4):
        from_x(e)
    pl.semaphore_wait(known, 3)
    for t in range(8):
        tile_copy(t).wait()
    arrived(seg.at[pl.ds(0, 96), :], recv_sem.at[1])
    for jp in range(2):
        turned = lax.dot_general(
            foldhot[jp], seg[...], (((1,), (1,)), ((), ())), preferred_element_type=F32
        )
        seg_t[jp] = turned.astype(BF16)
    arrived(xw.at[pl.ds(0, 16)], recv_sem.at[0])

    x_ref[...] = jnp.dot(colhot[...], xw[...].reshape(512, 512), preferred_element_type=F32)
    for t in range(8):
        products(t, x_ref, tile_vm, z_ref)

    sums = [jnp.dot(rowhot[...], z_ref[jp], preferred_element_type=F32) for jp in range(2)]
    cross = jnp.zeros((256, 256), F32)
    for jp in range(2):
        for half in in_two(sums[jp]):
            cross = cross + jnp.dot(seg_t[jp], half, preferred_element_type=F32)
    group = iota((8, 128), 1) // 8
    packed = gsum[...]
    for c in range(32):
        block = cross[8 * c : 8 * c + 8, 128 * (c // 16) : 128 * (c // 16) + 128]
        packed = packed + jnp.where(group == c % 16, block, 0.0)
    packed = group_sum(packed)

    at_a, at_b = x * 4 + y, z * 2 + core
    stage_a[at_a] = packed
    far_first = (10, 11, 9, 14, 6, 2, 8, 15, 13, 7, 5, 3, 1, 12, 4)
    for d in far_first:
        remote(stage_a.at[at_a], stage_a.at[at_a], send_sem.at[3], recv_sem.at[3], plane_peer[d]).start()

    total = None
    for jp in range(2):
        for half in in_two(sums[jp]):
            term = jnp.dot(half, foldhot[jp], preferred_element_type=F32)
            total = term if total is None else total + term
    partial32[...] = total
    for p in range(4):
        outgoing[:, p] = total[:, 128 * p : 128 * p + 128].astype(BF16).reshape(8, 16, 128)
    for d in range(1, 8):
        to = (col + d) % 8
        remote(outgoing.at[to], incoming.at[col], send_sem.at[2], recv_sem.at[2], (row, to)).start()

    arrived(stage_a.at[pl.ds(0, 15)], recv_sem.at[3])
    stage_b[at_b] = stage_a[...].sum(axis=0)
    far_first = (8, 9, 6, 7, 10, 11, 4, 5, 12, 13, 2, 3, 14, 15, 1)
    for d in far_first:
        remote(stage_b.at[at_b], stage_b.at[at_b], send_sem.at[4], recv_sem.at[4], line_peer[d]).start()

    sent(xw.at[pl.ds(0, 31)], 0)
    sent(seg.at[pl.ds(0, 112), :], 1)
    sent(outgoing.at[pl.ds(0, 7)], 2)
    sent(stage_a.at[pl.ds(0, 15)], 3)

    arrived(incoming.at[pl.ds(0, 7)], recv_sem.at[2])
    incoming[col] = jnp.zeros((4, 16, 128), BF16)
    own_rows = pl.ds(pl.multiple_of(16 * col, 16), 16)
    for p in range(4):
        share_p = partial32[own_rows, 128 * p : 128 * p + 128]
        for c in range(8):
            share_p = share_p + incoming[c, p].astype(F32)
        from_blocks(share_p, p, shares)
    whole = natural[...] + shares[...]
    whole_ref[...] = whole

    arrived(stage_b.at[pl.ds(0, 15)], recv_sem.at[4])
    gram = stage_b[...].sum(axis=0) / n_states
    same = iota((8, 128), 0) == iota((8, 128), 1)
    along = jnp.zeros((8, 1024), F32)
    for a in range(8):
        coef = jnp.where(same, gram[a : a + 1], 0.0).sum(axis=1, keepdims=True)
        along = along + coef * own[a : a + 1]
    along_ref[...] = along
    sent(stage_b.at[pl.ds(0, 15)], 4)


def per_device(vectors, energies, tiles, tile_rows, tile_cols, tile_count):
    n_states = 32 * 8 * 1024
    stored = tiles.reshape(128, 8, 32, 128).transpose(0, 2, 1, 3).reshape(8, 4096, 128)
    vmem = pl.BlockSpec(memory_space=pltpu.VMEM)
    hbm = pl.BlockSpec(memory_space=pltpu.HBM)
    dma = pltpu.SemaphoreType.DMA
    whole, along = pl.pallas_call(
        lambda *refs: kernel(n_states, *refs),
        out_shape=(
            jax.ShapeDtypeStruct((8, 1024), F32),
            jax.ShapeDtypeStruct((8, 1024), F32),
        ),
        in_specs=[hbm, hbm, hbm, hbm, hbm, pl.BlockSpec(memory_space=pltpu.SMEM)],
        out_specs=(vmem, vmem),
        scratch_shapes=[
            pltpu.VMEM((8, 1024), BF16),
            pltpu.VMEM((8, 128), F32),
            pltpu.VMEM((8, 128), jnp.int32),
            pltpu.VMEM((8, 128), jnp.int32),
            pltpu.VMEM((8, 4096, 128), BF16),
            pltpu.VMEM((32, 16, 512), BF16),
            pltpu.VMEM((128, 512), BF16),
            pltpu.VMEM((128, 1024), BF16),
            pltpu.VMEM((1024, 512), BF16),
            pltpu.VMEM((2, 256, 512), BF16),
            pltpu.VMEM((1024, 512), F32),
            pltpu.VMEM((2, 1024, 256), BF16),
            pltpu.VMEM((16, 512), F32),
            pltpu.VMEM((128, 512), F32),
            pltpu.VMEM((8, 4, 16, 128), BF16),
            pltpu.VMEM((8, 4, 16, 128), BF16),
            pltpu.VMEM((8, 128), F32),
            pltpu.VMEM((2, 256, 128), BF16),
            pltpu.VMEM((8, 1024), F32),
            pltpu.VMEM((16, 8, 128), F32),
            pltpu.VMEM((16, 8, 128), F32),
            pltpu.VMEM((8, 1024), F32),
            dma((4,)),
            dma((8,)),
            dma((8,)),
            dma((9,)),
            dma((5,)),
            dma((5,)),
            pltpu.SemaphoreType.REGULAR,
        ],
        compiler_params=pltpu.CompilerParams(
            collective_id=0, has_side_effects=True, vmem_limit_bytes=48 * 2**20
        ),
    )(
        *(
            pltpu.with_memory_space_constraint(value, pltpu.HBM)
            for value in (
                vectors,
                energies.reshape(8, 128),
                stored,
                tile_rows.reshape(8, 128),
                tile_cols.reshape(8, 128),
            )
        ),
        tile_count,
    )
    return whole.astype(BF16), whole - along


def solution(mesh):
    in_specs = (
        P(None, ("row", "col")),
        P(("row", "col")),
        P(("row", "col"), None),
        P(("row", "col")),
        P(("row", "col")),
        P(("row", "col")),
    )
    out_specs = (P(None, ("row", "col")), P(None, ("row", "col")))
    return jax.shard_map(
        per_device, mesh=mesh, in_specs=in_specs, out_specs=out_specs, check_vma=False
    )
```

```python
import jax
import jax.numpy as jnp
from jax import lax
from jax.experimental import pallas as pl
from jax.experimental.pallas import tpu as pltpu
from jax.sharding import PartitionSpec as P

F32, BF16 = jnp.float32, jnp.bfloat16


def iota(shape, dim):
    return lax.broadcasted_iota(jnp.int32, shape, dim)


def low_half():
    return iota((1, 128), 1) < 64


def turn(value):
    return pltpu.roll(value, 64, 1)


def to_blocks(natural, out_ref):
    low = low_half()
    for t in range(8):
        part = natural[:, 128 * t : 128 * t + 128]
        turned = turn(part)
        for p in range(4):
            a, b = 2 * p, 2 * p + 1
            lanes = pl.ds(128 * p, 128)
            out_ref[pl.ds(2 * t, 1), lanes] = jnp.where(low, part[a : a + 1], turned[b : b + 1])
            out_ref[pl.ds(2 * t + 1, 1), lanes] = jnp.where(low, turned[a : a + 1], part[b : b + 1])


def from_blocks(value, p, out_ref):
    low = low_half()
    turned = turn(value)
    for t in range(8):
        a, b = 2 * t, 2 * t + 1
        lanes = pl.ds(128 * t, 128)
        out_ref[pl.ds(2 * p, 1), lanes] = jnp.where(low, value[a : a + 1], turned[b : b + 1])
        out_ref[pl.ds(2 * p + 1, 1), lanes] = jnp.where(low, turned[a : a + 1], value[b : b + 1])


def mirrored(value):
    lane = iota(value.shape, 1)
    for bit in (1, 2, 4):
        swapped = jnp.where((lane & bit) != 0, pltpu.roll(value, bit, 1), pltpu.roll(value, 128 - bit, 1))
        value = swapped
    return value


def onehots(rows_ref, cols_ref, count_ref, rowhot, colhot, foldhot):
    count = count_ref[0]
    slot = iota((8, 128), 0) * 128 + iota((8, 128), 1)
    rows = mirrored(jnp.where(slot < count, rows_ref[...], -1))
    cols = jnp.transpose(mirrored(cols_ref[...]).astype(F32))
    row_ids = iota((128, 128), 0)
    col_ids = iota((128, 512), 1).astype(F32)
    for t in range(8):
        hot = row_ids == rows[t : t + 1, :]
        rowhot[:, 128 * t : 128 * t + 128] = jnp.where(hot, 1.0, 0.0).astype(BF16)
        hot = cols[:, t : t + 1] == col_ids
        colhot[128 * t : 128 * t + 128, :] = jnp.where(hot, 1.0, 0.0).astype(BF16)
    at = iota((256, 512), 0)
    spot = 64 * (at % 8) + 2 * (at // 8)
    lane = iota((256, 512), 1)
    for jp in range(2):
        foldhot[jp] = jnp.where(lane == spot + jp, 1.0, 0.0).astype(BF16)


def products(t, x_ref, tile_ref, z_ref):
    low = low_half()
    parts = []
    for jp in range(2):
        keep = low if jp == 0 else jnp.logical_not(low)
        for k in range(8):
            value = x_ref[pl.ds(128 * t, 128), 128 * (k // 2) : 128 * (k // 2) + 128]
            if k % 2 != jp:
                value = turn(value)
            parts.append(jnp.where(keep, value, 0.0))
    away = (iota((8, 128), 1) + iota((8, 128), 0) + 1) % 8
    outs = []
    for g in range(16):
        left = jnp.concatenate([part[8 * g : 8 * g + 8] for part in parts], axis=0).astype(BF16)
        right = tile_ref[t, pl.ds(256 * g, 256), :]
        out = lax.dot_general(left, right, (((1,), (1,)), ((), ())), preferred_element_type=F32)
        merged = []
        for jp in range(2):
            for h in range(2):
                lanes = slice(128 * h, 128 * h + 128)
                both = out[64 * jp : 64 * jp + 8, lanes]
                for k in range(1, 8):
                    first = 64 * jp + 8 * k
                    moved = pltpu.roll(out[first : first + 8, lanes], k, 1)
                    both = jnp.where(away == k, moved, both)
                merged.append(pltpu.roll(both, 121, 1, stride=1, stride_axis=0))
        outs.append(merged)
        if g % 2 == 1:
            first = 128 * t + 8 * (g - 1)
            for jp in range(2):
                for h in range(2):
                    pair = [o[2 * jp + h] for o in outs]
                    z_ref[jp, pl.ds(first, 16), 128 * h : 128 * h + 128] = jnp.concatenate(pair, axis=0).astype(BF16)
            outs = []


def in_two(value):
    upper = value.astype(BF16)
    return upper, (value - upper.astype(F32)).astype(BF16)


def group_sum(value):
    for shift in (64, 32, 16, 8):
        value = value + pltpu.roll(value, shift, 1)
    return value


def kernel(
    n_states,
    vectors_ref,
    energies_ref,
    tiles_ref,
    rows_ref,
    cols_ref,
    count_ref,
    whole_ref,
    along_ref,
    vectors_vm,
    energies_vm,
    rows_vm,
    cols_vm,
    tile_vm,
    xw,
    seg,
    rowhot,
    colhot,
    foldhot,
    x_ref,
    z_ref,
    own32,
    partial32,
    outgoing,
    incoming,
    gsum,
    seg_t,
    shares,
    stage_a,
    stage_b,
    natural,
    in_sem,
    tile_sem,
    z_recv,
    x_recv,
    send_sem,
    recv_sem,
    known,
):
    row, col = lax.axis_index("row"), lax.axis_index("col")
    core, xl, z = row % 2, (row // 2) % 2, row // 4
    xh, y = col % 2, col // 2
    low = low_half()

    def at(z_at, x_at, core_at, y_at):
        return (z_at * 2 + x_at % 2) * 2 + core_at, y_at * 2 + x_at // 2

    x = xh * 2 + xl
    z_peer = [at((z + d) % 8, x, core, y) for d in range(8)]
    x_peer = [at(z, (x + d) % 4, core, y) for d in range(4)]
    y_peer = [at(z, x, core, (y + d) % 4) for d in range(4)]
    here = at(z, x, 1 - core, y)
    across = at(z, xh * 2 + 1 - xl, core, y)
    plane_peer = [at(z, (x + d // 4) % 4, core, (y + d % 4) % 4) for d in range(16)]
    line_peer = [at((z + d // 2) % 8, x, (core + d) % 2, y) for d in range(16)]
    mesh_ids = pl.DeviceIdType.MESH

    barrier = pltpu.get_barrier_semaphore()
    near = (z_peer[2], z_peer[6], x_peer[2], y_peer[2], z_peer[1], z_peer[7])
    near = near + (x_peer[1], x_peer[3], y_peer[1], y_peer[3], here)

    loads = [
        pltpu.make_async_copy(src, dst, in_sem.at[i])
        for i, (src, dst) in enumerate(
            (
                (vectors_ref, vectors_vm),
                (cols_ref, cols_vm),
                (rows_ref, rows_vm),
                (energies_ref, energies_vm),
            )
        )
    ]
    loads[0].start()
    for peer in near:
        pl.semaphore_signal(barrier, inc=1, device_id=peer, device_id_type=mesh_ids)

    def tile_copy(t):
        return pltpu.make_async_copy(tiles_ref.at[t], tile_vm.at[t], tile_sem.at[t])

    mine = seg.at[pl.ds(pl.multiple_of(16 * col, 16), 16), :]
    loads[0].wait()
    own = vectors_vm[...].astype(F32)
    to_blocks(own, own32)
    xw[row] = own32[...].astype(BF16)
    mine[...] = own32[...].astype(BF16)

    pl.semaphore_wait(barrier, len(near))

    def remote(src, dst, send, recv, peer):
        return pltpu.make_async_remote_copy(
            src_ref=src,
            dst_ref=dst,
            send_sem=send,
            recv_sem=recv,
            device_id=peer,
            device_id_type=mesh_ids,
        )

    def arrived(ref, recv):
        remote(ref, ref, send_sem.at[0], recv, here).wait_recv()

    def sent(ref, i):
        remote(ref, ref, send_sem.at[i], recv_sem.at[i], here).wait_send()

    def pass_on(piece, recv, peer):
        remote(xw.at[piece], xw.at[piece], send_sem.at[0], recv, peer).start()

    def to_x_and_core(piece, e):
        pass_on(piece, x_recv.at[e], across)
        pass_on(piece, recv_sem.at[0], here)

    for d in (2, 6, 1, 7):
        pass_on(row, z_recv.at[8 - d], z_peer[d])
    to_x_and_core(row, 0)

    def share(ref, recv, peer):
        remote(ref, ref, send_sem.at[1], recv, peer).start()

    share(mine, x_recv.at[8], x_peer[2])
    for d in (2, 1, 3):
        pl.semaphore_signal(known, inc=1, device_id=y_peer[d], device_id_type=mesh_ids)
        share(mine, recv_sem.at[1], y_peer[d])

    for load in loads[1:]:
        load.start()
    for t in range(8):
        tile_copy(t).start()
    further = {1: (6, 3), 7: (2, 5), 2: (6, 4)}

    def from_z(e):
        piece = z_peer[e][0]
        arrived(xw.at[piece], z_recv.at[e])
        if e in further:
            d, there = further[e]
            pass_on(piece, z_recv.at[there], z_peer[d])
        to_x_and_core(piece, e)

    def from_x(e):
        piece = at((z + e) % 8, xh * 2 + 1 - xl, core, y)[0]
        arrived(xw.at[piece], x_recv.at[e])
        pass_on(piece, recv_sem.at[0], here)

    for e in (1, 7, 2, 6):
        from_z(e)
    for load in loads[1:]:
        load.wait()
    onehots(rows_vm, cols_vm, count_ref, rowhot, colhot, foldhot)
    energies = energies_vm[...]
    diag = [own[:, 128 * t : 128 * t + 128] * energies[t : t + 1] for t in range(8)]
    diag = jnp.concatenate(diag, axis=1)
    natural[...] = diag
    upper = diag.astype(BF16).astype(F32)
    halves = jnp.concatenate([upper, diag - upper, jnp.zeros((112, 1024), F32)], axis=0)
    gsum[...] = lax.dot_general(
        vectors_vm[...], halves.astype(BF16), (((1,), (1,)), ((), ())), preferred_element_type=F32
    )

    theirs = seg.at[pl.ds(pl.multiple_of(16 * (2 * y + 1 - xh), 16), 16), :]
    arrived(theirs, x_recv.at[8])
    for d in (2, 1, 3):
        share(theirs, recv_sem.at[1], y_peer[d])
    for e in (0, 1, 7):
        from_x(e)
    for e in (3, 5, 4):
        from_z(e)
    for e in (2, 6, 3, 5, 4):
        from_x(e)
    pl.semaphore_wait(known, 3)
    for t in range(8):
        tile_copy(t).wait()
    arrived(seg.at[pl.ds(0, 96), :], recv_sem.at[1])
    for jp in range(2):
        turned = lax.dot_general(
            foldhot[jp], seg[...], (((1,), (1,)), ((), ())), preferred_element_type=F32
        )
        seg_t[jp] = turned.astype(BF16)
    arrived(xw.at[pl.ds(0, 16)], recv_sem.at[0])

    x_ref[...] = jnp.dot(colhot[...], xw[...].reshape(512, 512), preferred_element_type=F32)
    for t in range(8):
        products(t, x_ref, tile_vm, z_ref)

    sums = [jnp.dot(rowhot[...], z_ref[jp], preferred_element_type=F32) for jp in range(2)]
    cross = jnp.zeros((256, 256), F32)
    for jp in range(2):
        for half in in_two(sums[jp]):
            cross = cross + jnp.dot(seg_t[jp], half, preferred_element_type=F32)
    group = iota((8, 128), 1) // 8
    packed = gsum[...]
    for c in range(32):
        block = cross[8 * c : 8 * c + 8, 128 * (c // 16) : 128 * (c // 16) + 128]
        packed = packed + jnp.where(group == c % 16, block, 0.0)
    packed = group_sum(packed)

    at_a, at_b = x * 4 + y, z * 2 + core
    stage_a[at_a] = packed
    far_first = (10, 11, 9, 14, 6, 2, 8, 15, 13, 7, 5, 3, 1, 12, 4)
    for d in far_first:
        remote(stage_a.at[at_a], stage_a.at[at_a], send_sem.at[3], recv_sem.at[3], plane_peer[d]).start()

    total = None
    for jp in range(2):
        for half in in_two(sums[jp]):
            term = jnp.dot(half, foldhot[jp], preferred_element_type=F32)
            total = term if total is None else total + term
    partial32[...] = total
    for p in range(4):
        outgoing[:, p] = total[:, 128 * p : 128 * p + 128].astype(BF16).reshape(8, 16, 128)
    for d in range(1, 8):
        to = (col + d) % 8
        remote(outgoing.at[to], incoming.at[col], send_sem.at[2], recv_sem.at[2], (row, to)).start()

    arrived(stage_a.at[pl.ds(0, 15)], recv_sem.at[3])
    stage_b[at_b] = stage_a[...].sum(axis=0)
    far_first = (8, 9, 6, 7, 10, 11, 4, 5, 12, 13, 2, 3, 14, 15, 1)
    for d in far_first:
        remote(stage_b.at[at_b], stage_b.at[at_b], send_sem.at[4], recv_sem.at[4], line_peer[d]).start()

    sent(xw.at[pl.ds(0, 31)], 0)
    sent(seg.at[pl.ds(0, 112), :], 1)
    sent(outgoing.at[pl.ds(0, 7)], 2)
    sent(stage_a.at[pl.ds(0, 15)], 3)

    arrived(incoming.at[pl.ds(0, 7)], recv_sem.at[2])
    incoming[col] = jnp.zeros((4, 16, 128), BF16)
    own_rows = pl.ds(pl.multiple_of(16 * col, 16), 16)
    for p in range(4):
        share_p = partial32[own_rows, 128 * p : 128 * p + 128]
        for c in range(8):
            share_p = share_p + incoming[c, p].astype(F32)
        from_blocks(share_p, p, shares)
    whole = natural[...] + shares[...]
    whole_ref[...] = whole

    arrived(stage_b.at[pl.ds(0, 15)], recv_sem.at[4])
    gram = stage_b[...].sum(axis=0) / n_states
    same = iota((8, 128), 0) == iota((8, 128), 1)
    along = jnp.zeros((8, 1024), F32)
    for a in range(8):
        coef = jnp.where(same, gram[a : a + 1], 0.0).sum(axis=1, keepdims=True)
        along = along + coef * own[a : a + 1]
    along_ref[...] = along
    sent(stage_b.at[pl.ds(0, 15)], 4)


def per_device(vectors, energies, tiles, tile_rows, tile_cols, tile_count):
    n_states = 32 * 8 * 1024
    stored = tiles.reshape(128, 8, 32, 128).transpose(0, 2, 1, 3).reshape(8, 4096, 128)
    vmem = pl.BlockSpec(memory_space=pltpu.VMEM)
    hbm = pl.BlockSpec(memory_space=pltpu.HBM)
    dma = pltpu.SemaphoreType.DMA
    whole, along = pl.pallas_call(
        lambda *refs: kernel(n_states, *refs),
        out_shape=(
            jax.ShapeDtypeStruct((8, 1024), F32),
            jax.ShapeDtypeStruct((8, 1024), F32),
        ),
        in_specs=[hbm, hbm, hbm, hbm, hbm, pl.BlockSpec(memory_space=pltpu.SMEM)],
        out_specs=(vmem, vmem),
        scratch_shapes=[
            pltpu.VMEM((8, 1024), BF16),
            pltpu.VMEM((8, 128), F32),
            pltpu.VMEM((8, 128), jnp.int32),
            pltpu.VMEM((8, 128), jnp.int32),
            pltpu.VMEM((8, 4096, 128), BF16),
            pltpu.VMEM((32, 16, 512), BF16),
            pltpu.VMEM((128, 512), BF16),
            pltpu.VMEM((128, 1024), BF16),
            pltpu.VMEM((1024, 512), BF16),
            pltpu.VMEM((2, 256, 512), BF16),
            pltpu.VMEM((1024, 512), F32),
            pltpu.VMEM((2, 1024, 256), BF16),
            pltpu.VMEM((16, 512), F32),
            pltpu.VMEM((128, 512), F32),
            pltpu.VMEM((8, 4, 16, 128), BF16),
            pltpu.VMEM((8, 4, 16, 128), BF16),
            pltpu.VMEM((8, 128), F32),
            pltpu.VMEM((2, 256, 128), BF16),
            pltpu.VMEM((8, 1024), F32),
            pltpu.VMEM((16, 8, 128), F32),
            pltpu.VMEM((16, 8, 128), F32),
            pltpu.VMEM((8, 1024), F32),
            dma((4,)),
            dma((8,)),
            dma((8,)),
            dma((9,)),
            dma((5,)),
            dma((5,)),
            pltpu.SemaphoreType.REGULAR,
        ],
        compiler_params=pltpu.CompilerParams(
            collective_id=0, has_side_effects=True, vmem_limit_bytes=48 * 2**20
        ),
    )(
        *(
            pltpu.with_memory_space_constraint(value, pltpu.HBM)
            for value in (
                vectors,
                energies.reshape(8, 128),
                stored,
                tile_rows.reshape(8, 128),
                tile_cols.reshape(8, 128),
            )
        ),
        tile_count,
    )
    return whole.astype(BF16), whole - along


def solution(mesh):
    in_specs = (
        P(None, ("row", "col")),
        P(("row", "col")),
        P(("row", "col"), None),
        P(("row", "col")),
        P(("row", "col")),
        P(("row", "col")),
    )
    out_specs = (P(None, ("row", "col")), P(None, ("row", "col")))
    return jax.shard_map(
        per_device, mesh=mesh, in_specs=in_specs, out_specs=out_specs, check_vma=False
    )
```

```python
import jax
import jax.numpy as jnp
from jax import lax
from jax.experimental import pallas as pl
from jax.experimental.pallas import tpu as pltpu
from jax.sharding import PartitionSpec as P

F32, BF16 = jnp.float32, jnp.bfloat16


def iota(shape, dim):
    return lax.broadcasted_iota(jnp.int32, shape, dim)


def low_half():
    return iota((1, 128), 1) < 64


def turn(value):
    return pltpu.roll(value, 64, 1)


def to_blocks(natural, out_ref):
    low = low_half()
    for t in range(8):
        part = natural[:, 128 * t : 128 * t + 128]
        turned = turn(part)
        for p in range(4):
            a, b = 2 * p, 2 * p + 1
            lanes = pl.ds(128 * p, 128)
            out_ref[pl.ds(2 * t, 1), lanes] = jnp.where(low, part[a : a + 1], turned[b : b + 1])
            out_ref[pl.ds(2 * t + 1, 1), lanes] = jnp.where(low, turned[a : a + 1], part[b : b + 1])


def from_blocks(value, p, out_ref):
    low = low_half()
    turned = turn(value)
    for t in range(8):
        a, b = 2 * t, 2 * t + 1
        lanes = pl.ds(128 * t, 128)
        out_ref[pl.ds(2 * p, 1), lanes] = jnp.where(low, value[a : a + 1], turned[b : b + 1])
        out_ref[pl.ds(2 * p + 1, 1), lanes] = jnp.where(low, turned[a : a + 1], value[b : b + 1])


def mirrored(value):
    lane = iota(value.shape, 1)
    for bit in (1, 2, 4):
        swapped = jnp.where((lane & bit) != 0, pltpu.roll(value, bit, 1), pltpu.roll(value, 128 - bit, 1))
        value = swapped
    return value


def onehots(rows_ref, cols_ref, count_ref, rowhot, colhot, foldhot):
    count = count_ref[0]
    slot = iota((8, 128), 0) * 128 + iota((8, 128), 1)
    rows = mirrored(jnp.where(slot < count, rows_ref[...], -1))
    cols = jnp.transpose(mirrored(cols_ref[...]).astype(F32))
    row_ids = iota((128, 128), 0)
    col_ids = iota((128, 512), 1).astype(F32)
    for t in range(8):
        hot = row_ids == rows[t : t + 1, :]
        rowhot[:, 128 * t : 128 * t + 128] = jnp.where(hot, 1.0, 0.0).astype(BF16)
        hot = cols[:, t : t + 1] == col_ids
        colhot[128 * t : 128 * t + 128, :] = jnp.where(hot, 1.0, 0.0).astype(BF16)
    at = iota((256, 512), 0)
    spot = 64 * (at % 8) + 2 * (at // 8)
    lane = iota((256, 512), 1)
    for jp in range(2):
        foldhot[jp] = jnp.where(lane == spot + jp, 1.0, 0.0).astype(BF16)


def products(t, x_ref, tile_ref, z_ref):
    low = low_half()
    parts = []
    for jp in range(2):
        keep = low if jp == 0 else jnp.logical_not(low)
        for k in range(8):
            value = x_ref[pl.ds(128 * t, 128), 128 * (k // 2) : 128 * (k // 2) + 128]
            if k % 2 != jp:
                value = turn(value)
            parts.append(jnp.where(keep, value, 0.0))
    away = (iota((8, 128), 1) + iota((8, 128), 0) + 1) % 8
    outs = []
    for g in range(16):
        left = jnp.concatenate([part[8 * g : 8 * g + 8] for part in parts], axis=0).astype(BF16)
        right = tile_ref[t, pl.ds(256 * g, 256), :]
        out = lax.dot_general(left, right, (((1,), (1,)), ((), ())), preferred_element_type=F32)
        merged = []
        for jp in range(2):
            for h in range(2):
                lanes = slice(128 * h, 128 * h + 128)
                both = out[64 * jp : 64 * jp + 8, lanes]
                for k in range(1, 8):
                    first = 64 * jp + 8 * k
                    moved = pltpu.roll(out[first : first + 8, lanes], k, 1)
                    both = jnp.where(away == k, moved, both)
                merged.append(pltpu.roll(both, 121, 1, stride=1, stride_axis=0))
        outs.append(merged)
        if g % 2 == 1:
            first = 128 * t + 8 * (g - 1)
            for jp in range(2):
                for h in range(2):
                    pair = [o[2 * jp + h] for o in outs]
                    z_ref[jp, pl.ds(first, 16), 128 * h : 128 * h + 128] = jnp.concatenate(pair, axis=0).astype(BF16)
            outs = []


def in_two(value):
    upper = value.astype(BF16)
    return upper, (value - upper.astype(F32)).astype(BF16)


def group_sum(value):
    for shift in (64, 32, 16, 8):
        value = value + pltpu.roll(value, shift, 1)
    return value


def kernel(
    n_states,
    vectors_ref,
    energies_ref,
    tiles_ref,
    rows_ref,
    cols_ref,
    count_ref,
    whole_ref,
    along_ref,
    vectors_vm,
    energies_vm,
    rows_vm,
    cols_vm,
    tile_vm,
    xw,
    seg,
    rowhot,
    colhot,
    foldhot,
    x_ref,
    z_ref,
    own32,
    partial32,
    outgoing,
    incoming,
    gsum,
    seg_t,
    shares,
    stage_a,
    stage_b,
    natural,
    in_sem,
    tile_sem,
    z_recv,
    x_recv,
    send_sem,
    recv_sem,
    known,
):
    row, col = lax.axis_index("row"), lax.axis_index("col")
    core, xl, z = row % 2, (row // 2) % 2, row // 4
    xh, y = col % 2, col // 2
    low = low_half()

    def at(z_at, x_at, core_at, y_at):
        return (z_at * 2 + x_at % 2) * 2 + core_at, y_at * 2 + x_at // 2

    x = xh * 2 + xl
    z_peer = [at((z + d) % 8, x, core, y) for d in range(8)]
    x_peer = [at(z, (x + d) % 4, core, y) for d in range(4)]
    y_peer = [at(z, x, core, (y + d) % 4) for d in range(4)]
    here = at(z, x, 1 - core, y)
    across = at(z, xh * 2 + 1 - xl, core, y)
    plane_peer = [at(z, (x + d // 4) % 4, core, (y + d % 4) % 4) for d in range(16)]
    line_peer = [at((z + d // 2) % 8, x, (core + d) % 2, y) for d in range(16)]
    mesh_ids = pl.DeviceIdType.MESH

    barrier = pltpu.get_barrier_semaphore()
    near = (z_peer[2], z_peer[6], x_peer[2], y_peer[2], z_peer[1], z_peer[7])
    near = near + (x_peer[1], x_peer[3], y_peer[1], y_peer[3], here)

    loads = [
        pltpu.make_async_copy(src, dst, in_sem.at[i])
        for i, (src, dst) in enumerate(
            (
                (vectors_ref, vectors_vm),
                (cols_ref, cols_vm),
                (rows_ref, rows_vm),
                (energies_ref, energies_vm),
            )
        )
    ]
    loads[0].start()
    for peer in near:
        pl.semaphore_signal(barrier, inc=1, device_id=peer, device_id_type=mesh_ids)

    def tile_copy(t):
        return pltpu.make_async_copy(tiles_ref.at[t], tile_vm.at[t], tile_sem.at[t])

    mine = seg.at[pl.ds(pl.multiple_of(16 * col, 16), 16), :]
    loads[0].wait()
    own = vectors_vm[...].astype(F32)
    to_blocks(own, own32)
    xw[row] = own32[...].astype(BF16)
    mine[...] = own32[...].astype(BF16)

    pl.semaphore_wait(barrier, len(near))

    def remote(src, dst, send, recv, peer):
        return pltpu.make_async_remote_copy(
            src_ref=src,
            dst_ref=dst,
            send_sem=send,
            recv_sem=recv,
            device_id=peer,
            device_id_type=mesh_ids,
        )

    def arrived(ref, recv):
        remote(ref, ref, send_sem.at[0], recv, here).wait_recv()

    def sent(ref, i):
        remote(ref, ref, send_sem.at[i], recv_sem.at[i], here).wait_send()

    def pass_on(piece, recv, peer):
        remote(xw.at[piece], xw.at[piece], send_sem.at[0], recv, peer).start()

    def to_x_and_core(piece, e):
        pass_on(piece, x_recv.at[e], across)
        pass_on(piece, recv_sem.at[0], here)

    for d in (2, 6, 1, 7):
        pass_on(row, z_recv.at[8 - d], z_peer[d])
    to_x_and_core(row, 0)

    def share(ref, recv, peer):
        remote(ref, ref, send_sem.at[1], recv, peer).start()

    share(mine, x_recv.at[8], x_peer[2])
    for d in (2, 1, 3):
        pl.semaphore_signal(known, inc=1, device_id=y_peer[d], device_id_type=mesh_ids)
        share(mine, recv_sem.at[1], y_peer[d])

    for load in loads[1:]:
        load.start()
    for t in range(8):
        tile_copy(t).start()
    further = {1: (6, 3), 7: (2, 5), 2: (6, 4)}

    def from_z(e):
        piece = z_peer[e][0]
        arrived(xw.at[piece], z_recv.at[e])
        if e in further:
            d, there = further[e]
            pass_on(piece, z_recv.at[there], z_peer[d])
        to_x_and_core(piece, e)

    def from_x(e):
        piece = at((z + e) % 8, xh * 2 + 1 - xl, core, y)[0]
        arrived(xw.at[piece], x_recv.at[e])
        pass_on(piece, recv_sem.at[0], here)

    for e in (1, 7, 2, 6):
        from_z(e)
    for load in loads[1:]:
        load.wait()
    onehots(rows_vm, cols_vm, count_ref, rowhot, colhot, foldhot)
    energies = energies_vm[...]
    diag = [own[:, 128 * t : 128 * t + 128] * energies[t : t + 1] for t in range(8)]
    diag = jnp.concatenate(diag, axis=1)
    natural[...] = diag
    upper = diag.astype(BF16).astype(F32)
    halves = jnp.concatenate([upper, diag - upper, jnp.zeros((112, 1024), F32)], axis=0)
    gsum[...] = lax.dot_general(
        vectors_vm[...], halves.astype(BF16), (((1,), (1,)), ((), ())), preferred_element_type=F32
    )

    theirs = seg.at[pl.ds(pl.multiple_of(16 * (2 * y + 1 - xh), 16), 16), :]
    arrived(theirs, x_recv.at[8])
    for d in (2, 1, 3):
        share(theirs, recv_sem.at[1], y_peer[d])
    for e in (0, 1, 7):
        from_x(e)
    from_z(3)
    from_x(2)
    from_z(5)
    from_x(6)
    from_z(4)
    for e in (3, 5, 4):
        from_x(e)
    pl.semaphore_wait(known, 3)
    for t in range(8):
        tile_copy(t).wait()
    arrived(seg.at[pl.ds(0, 96), :], recv_sem.at[1])
    for jp in range(2):
        turned = lax.dot_general(
            foldhot[jp], seg[...], (((1,), (1,)), ((), ())), preferred_element_type=F32
        )
        seg_t[jp] = turned.astype(BF16)
    arrived(xw.at[pl.ds(0, 16)], recv_sem.at[0])

    x_ref[...] = jnp.dot(colhot[...], xw[...].reshape(512, 512), preferred_element_type=F32)
    for t in range(8):
        products(t, x_ref, tile_vm, z_ref)

    sums = [jnp.dot(rowhot[...], z_ref[jp], preferred_element_type=F32) for jp in range(2)]
    cross = jnp.zeros((256, 256), F32)
    for jp in range(2):
        for half in in_two(sums[jp]):
            cross = cross + jnp.dot(seg_t[jp], half, preferred_element_type=F32)
    group = iota((8, 128), 1) // 8
    packed = gsum[...]
    for c in range(32):
        block = cross[8 * c : 8 * c + 8, 128 * (c // 16) : 128 * (c // 16) + 128]
        packed = packed + jnp.where(group == c % 16, block, 0.0)
    packed = group_sum(packed)

    at_a, at_b = x * 4 + y, z * 2 + core
    stage_a[at_a] = packed
    far_first = (10, 11, 9, 14, 6, 2, 8, 15, 13, 7, 5, 3, 1, 12, 4)
    for d in far_first:
        remote(stage_a.at[at_a], stage_a.at[at_a], send_sem.at[3], recv_sem.at[3], plane_peer[d]).start()

    total = None
    for jp in range(2):
        for half in in_two(sums[jp]):
            term = jnp.dot(half, foldhot[jp], preferred_element_type=F32)
            total = term if total is None else total + term
    partial32[...] = total
    for p in range(4):
        outgoing[:, p] = total[:, 128 * p : 128 * p + 128].astype(BF16).reshape(8, 16, 128)
    for d in range(1, 8):
        to = (col + d) % 8
        remote(outgoing.at[to], incoming.at[col], send_sem.at[2], recv_sem.at[2], (row, to)).start()

    arrived(stage_a.at[pl.ds(0, 15)], recv_sem.at[3])
    stage_b[at_b] = stage_a[...].sum(axis=0)
    far_first = (8, 9, 6, 7, 10, 11, 4, 5, 12, 13, 2, 3, 14, 15, 1)
    for d in far_first:
        remote(stage_b.at[at_b], stage_b.at[at_b], send_sem.at[4], recv_sem.at[4], line_peer[d]).start()

    sent(xw.at[pl.ds(0, 31)], 0)
    sent(seg.at[pl.ds(0, 112), :], 1)
    sent(outgoing.at[pl.ds(0, 7)], 2)
    sent(stage_a.at[pl.ds(0, 15)], 3)

    arrived(incoming.at[pl.ds(0, 7)], recv_sem.at[2])
    incoming[col] = jnp.zeros((4, 16, 128), BF16)
    own_rows = pl.ds(pl.multiple_of(16 * col, 16), 16)
    for p in range(4):
        share_p = partial32[own_rows, 128 * p : 128 * p + 128]
        for c in range(8):
            share_p = share_p + incoming[c, p].astype(F32)
        from_blocks(share_p, p, shares)
    whole = natural[...] + shares[...]
    whole_ref[...] = whole

    arrived(stage_b.at[pl.ds(0, 15)], recv_sem.at[4])
    gram = stage_b[...].sum(axis=0) / n_states
    same = iota((8, 128), 0) == iota((8, 128), 1)
    along = jnp.zeros((8, 1024), F32)
    for a in range(8):
        coef = jnp.where(same, gram[a : a + 1], 0.0).sum(axis=1, keepdims=True)
        along = along + coef * own[a : a + 1]
    along_ref[...] = along
    sent(stage_b.at[pl.ds(0, 15)], 4)


def per_device(vectors, energies, tiles, tile_rows, tile_cols, tile_count):
    n_states = 32 * 8 * 1024
    stored = tiles.reshape(128, 8, 32, 128).transpose(0, 2, 1, 3).reshape(8, 4096, 128)
    vmem = pl.BlockSpec(memory_space=pltpu.VMEM)
    hbm = pl.BlockSpec(memory_space=pltpu.HBM)
    dma = pltpu.SemaphoreType.DMA
    whole, along = pl.pallas_call(
        lambda *refs: kernel(n_states, *refs),
        out_shape=(
            jax.ShapeDtypeStruct((8, 1024), F32),
            jax.ShapeDtypeStruct((8, 1024), F32),
        ),
        in_specs=[hbm, hbm, hbm, hbm, hbm, pl.BlockSpec(memory_space=pltpu.SMEM)],
        out_specs=(vmem, vmem),
        scratch_shapes=[
            pltpu.VMEM((8, 1024), BF16),
            pltpu.VMEM((8, 128), F32),
            pltpu.VMEM((8, 128), jnp.int32),
            pltpu.VMEM((8, 128), jnp.int32),
            pltpu.VMEM((8, 4096, 128), BF16),
            pltpu.VMEM((32, 16, 512), BF16),
            pltpu.VMEM((128, 512), BF16),
            pltpu.VMEM((128, 1024), BF16),
            pltpu.VMEM((1024, 512), BF16),
            pltpu.VMEM((2, 256, 512), BF16),
            pltpu.VMEM((1024, 512), F32),
            pltpu.VMEM((2, 1024, 256), BF16),
            pltpu.VMEM((16, 512), F32),
            pltpu.VMEM((128, 512), F32),
            pltpu.VMEM((8, 4, 16, 128), BF16),
            pltpu.VMEM((8, 4, 16, 128), BF16),
            pltpu.VMEM((8, 128), F32),
            pltpu.VMEM((2, 256, 128), BF16),
            pltpu.VMEM((8, 1024), F32),
            pltpu.VMEM((16, 8, 128), F32),
            pltpu.VMEM((16, 8, 128), F32),
            pltpu.VMEM((8, 1024), F32),
            dma((4,)),
            dma((8,)),
            dma((8,)),
            dma((9,)),
            dma((5,)),
            dma((5,)),
            pltpu.SemaphoreType.REGULAR,
        ],
        compiler_params=pltpu.CompilerParams(
            collective_id=0, has_side_effects=True, vmem_limit_bytes=48 * 2**20
        ),
    )(
        *(
            pltpu.with_memory_space_constraint(value, pltpu.HBM)
            for value in (
                vectors,
                energies.reshape(8, 128),
                stored,
                tile_rows.reshape(8, 128),
                tile_cols.reshape(8, 128),
            )
        ),
        tile_count,
    )
    return whole.astype(BF16), whole - along


def solution(mesh):
    in_specs = (
        P(None, ("row", "col")),
        P(("row", "col")),
        P(("row", "col"), None),
        P(("row", "col")),
        P(("row", "col")),
        P(("row", "col")),
    )
    out_specs = (P(None, ("row", "col")), P(None, ("row", "col")))
    return jax.shard_map(
        per_device, mesh=mesh, in_specs=in_specs, out_specs=out_specs, check_vma=False
    )
```
